128 devices in a mesh: region: 8 (over x, core), dom: 16 (over y, z).
Axes of the slice: x: 4, y: 4, z: 4, core: 2. Of those that a mesh axis runs over, the one named last changes fastest.
Arguments:
- embeds: bfloat16 [262144, 256], P(('region', 'dom')), may hold values from -6 to 6
- neighbours: int32 [262144, 8], P(('region', 'dom')), may hold values from 0 to 4095
- halo_send: int32 [2048, 128], P(('region', 'dom')), may hold values from 0 to 2047
- gnn_weight: bfloat16 [512, 256], replicated, may hold values from -0.25 to 0.25
- pair_local: int32 [1024, 512], P(('region', 'dom')), may hold values from 0 to 2047
- pair_remote: int32 [1024, 512], P(('region', 'dom')), may hold values from 0 to 2047
- pair_count: int32 [128, 8], P(('region', 'dom')), may hold values from 1 to 512, as said below
- targets: float32 [1024, 512], P(('region', 'dom')), may hold values from -6 to 6
- pair_w1: bfloat16 [512, 256], replicated, may hold values from -0.25 to 0.25
- pair_w2: bfloat16 [256], replicated, may hold values from -0.375 to 0.375
Outputs:
- embeds_grad: bfloat16 [262144, 256], P(('region', 'dom'))
- gnn_grad: float32 [512, 256], replicated
- pair_w1_grad: float32 [512, 256], replicated
- pair_w2_grad: float32 [256], replicated
- loss: float32 [], replicated
The draws below stay inside these ranges and needn't reach their ends.
Inputs may be any that keep to these rules, and one draw needn't show every extreme that they name: `pair_count`: some partition has 512 live slots for some owner region in every draw.
All inputs are finite; a program needn't handle non-finite values.
Results may differ from the reference program's by a relative error of at most 0.0061.
Values may be sent and summed in bfloat16 or wider, within the bound.
A program may use at most 128 MiB of HBM per device.

```python
import math
import jax
import jax.numpy as jnp
import numpy as np
from jax import lax

NET_DEV = 2048
F = 256
HID = 256
DEG = 8
HALO = 128
CAP = 512
NETS = 262144
N_REGION = 8
N_DOM = 16


def draw_pair_count(key, part):
    devices = N_REGION * N_DOM
    rank = jnp.arange(devices, dtype=jnp.int32)[:, None]
    upper = CAP // 3 + (CAP - CAP // 3) * rank // (devices - 1) + 1
    lower = jnp.maximum(upper // 2, 1)
    first_key = jax.random.fold_in(key, 11)
    second_key = jax.random.fold_in(key, 12)
    third_key = jax.random.fold_in(key, 13)
    raw_bits = jax.random.randint(first_key, (devices, N_REGION), 0, 1 << 20)
    counts = lower + raw_bits % (upper - lower)
    heavy_device = jax.random.randint(second_key, (), devices // 2, devices)
    heavy_region = jax.random.randint(third_key, (), 0, N_REGION)
    counts = counts.at[heavy_device, heavy_region].set(CAP)
    return counts.astype(jnp.int32)


def with_ends(values, key, least, largest):
    extent = values.shape
    spot = [jax.random.randint(jax.random.fold_in(key, axis), (), 0, extent[axis]) for axis in range(len(extent))]
    values = values.at[tuple(spot)].set(least)
    longest = extent.index(max(extent))
    spot[longest] = (spot[longest] + 1) % extent[longest]
    return values.at[tuple(spot)].set(largest)


def block_levels(stream_key, dims, cuts, smallest, high):
    factor_of = 1.0
    for axis_at, blocks in cuts:
        draws = jax.random.uniform(jax.random.fold_in(jax.random.fold_in(stream_key, 6), axis_at), (blocks,), jnp.float32, smallest / len(cuts), high / len(cuts))
        factor_of = factor_of * jnp.repeat(jnp.exp(draws), dims[axis_at] // blocks).reshape((-1,) + (1,) * (len(dims) - 1 - axis_at))
    return factor_of


def rank_bounds(number_of, slope):
    portions = [(1 << 20) // math.isqrt(grade ** slope) + 1 for grade in range(1, number_of + 1)]
    deviation = 1 + sum(portions) // (1 << 30)
    return np.cumsum(np.array([max(1, weight // deviation) for weight in portions]))


def ranked(rng, dims, count, slope):
    listing = rank_bounds(count, slope)
    pick = jax.random.randint(jax.random.fold_in(rng, 1), dims, 0, int(listing[count - 1]))
    grade = jnp.searchsorted(jnp.asarray(listing, jnp.int32), pick, side="right")
    return jax.random.permutation(jax.random.fold_in(rng, 2), count)[grade].astype(jnp.int32)


def bell_draw(key, extent, spread, reach, pieces=(), held_as=jnp.bfloat16):
    result = spread * jax.random.normal(key, extent, jnp.float32)
    if pieces:
        result = result * block_levels(key, extent, pieces, -0.22, 0.18)
    return jnp.clip(result, -reach, reach).astype(held_as)


def setup_inputs(seed: int = 0) -> dict:
    seeds = jax.random.split(jax.random.key(seed), 11)
    return {
        "embeds": bell_draw(seeds[0], (NETS, F), 1.0, 6.0, ((0, 128),)),
        "neighbours": with_ends(jax.random.randint(seeds[1], (NETS, DEG), 0, NET_DEV + N_DOM * HALO), jax.random.fold_in(seeds[1], 1), 0, (NET_DEV + N_DOM * HALO) - 1).astype(jnp.int32),
        "halo_send": with_ends(jax.random.randint(seeds[2], (N_REGION * N_DOM * N_DOM, HALO), 0, NET_DEV), jax.random.fold_in(seeds[2], 1), 0, NET_DEV - 1).astype(jnp.int32),
        "gnn_weight": bell_draw(seeds[3], (2 * F, F), (2 * F) ** -0.5, 0.25),
        "pair_local": with_ends(jax.random.randint(seeds[4], (N_REGION * N_DOM * N_REGION, CAP), 0, NET_DEV), jax.random.fold_in(seeds[4], 1), 0, NET_DEV - 1).astype(jnp.int32),
        "pair_remote": with_ends(ranked(seeds[5], (N_REGION * N_DOM * N_REGION, CAP), NET_DEV, 2), jax.random.fold_in(seeds[5], 3), 0, NET_DEV - 1).astype(jnp.int32),
        "pair_count": draw_pair_count(jax.random.fold_in(seeds[10], 71), 0),
        "targets": bell_draw(seeds[7], (N_REGION * N_DOM * N_REGION, CAP), 1.0, 6.0, ((0, 128),), jnp.float32),
        "pair_w1": bell_draw(seeds[8], (2 * F, HID), (2 * F) ** -0.5, 0.25),
        "pair_w2": bell_draw(seeds[9], (HID,), HID ** -0.5, 0.375),
    }


gelu_coef = 0.7978845608

def gelu_tanh(value):
    inner = jnp.tanh(gelu_coef * (value + 0.044715 * value * value * value))
    return 0.5 * value * (1.0 + inner)

def gelu_slope(value):
    inner = jnp.tanh(gelu_coef * (value + 0.044715 * value * value * value))
    return 0.5 * (1.0 + inner) + 0.5 * value * (1.0 - inner * inner) * gelu_coef * (1.0 + 3.0 * 0.044715 * value * value)

def reference(embeds, neighbours, halo_send, gnn_weight, pair_local, pair_remote, pair_count, targets, pair_w1, pair_w2):
    regions = N_REGION
    doms = N_DOM
    devices = regions * doms
    own_blocks = embeds.reshape(devices, NET_DEV, F)
    neigh_blocks = neighbours.reshape(devices, NET_DEV, DEG)
    send_lists = halo_send.reshape(regions, doms, doms, HALO)
    local_blocks = pair_local.reshape(devices, regions, CAP)
    remote_blocks = pair_remote.reshape(devices, regions, CAP)
    target_blocks = targets.reshape(devices, regions * CAP)
    device_ids = jnp.arange(devices, dtype=jnp.int32)

    def lists_for(device):
        region_at = device // doms
        dom_at = device % doms
        lists = send_lists[region_at][:, dom_at, :]
        senders = region_at * doms + jnp.arange(doms, dtype=jnp.int32)
        return (senders, lists)

    def layer_inputs(device):
        senders, lists = lists_for(device)
        received = own_blocks[senders[:, None], lists]
        table = jnp.concatenate([own_blocks[device], received.reshape(-1, F)], 0)
        agg_sum = jnp.zeros((NET_DEV, F), jnp.float32)
        for column in range(DEG):
            agg_sum = agg_sum + table[neigh_blocks[device][:, column]].astype(jnp.float32)
        aggregate = (agg_sum / DEG).astype(jnp.bfloat16)
        joined = jnp.concatenate([own_blocks[device], aggregate], 1)
        pre = jnp.dot(joined, gnn_weight, preferred_element_type=jnp.float32)
        return (joined, pre)

    def forward(device):
        joined, pre = layer_inputs(device)
        return (own_blocks[device].astype(jnp.float32) + gelu_tanh(pre)).astype(jnp.bfloat16)
    net_blocks = lax.map(forward, device_ids)

    def pair_step(carry, device):
        dnets_all, grad_w1, grad_w2, sq_total = carry
        dom_at = device % doms
        owners = jnp.arange(regions, dtype=jnp.int32) * doms + dom_at
        partner = net_blocks[owners[:, None], remote_blocks[device]]
        victim = net_blocks[device][local_blocks[device]]
        pairs_in = jnp.concatenate([victim, partner], 2).reshape(regions * CAP, 2 * F)
        linear = jnp.dot(pairs_in, pair_w1, preferred_element_type=jnp.float32)
        activated = gelu_tanh(linear).astype(jnp.bfloat16)
        scores = jnp.dot(activated, pair_w2, preferred_element_type=jnp.float32)
        counts = pair_count[device]
        slot_ids = jnp.arange(CAP, dtype=jnp.int32)
        valid_mask = (slot_ids[None, :] < counts[:, None]).astype(jnp.float32).reshape(-1)
        errors = (scores - target_blocks[device]) * valid_mask
        residual = 2.0 * errors
        lin_grad = (residual[:, None] * pair_w2.astype(jnp.float32)[None, :] * gelu_slope(linear)).astype(jnp.bfloat16)
        grad_w1 = grad_w1 + jnp.dot(pairs_in.T, lin_grad, preferred_element_type=jnp.float32)
        grad_w2 = grad_w2 + lax.optimization_barrier(jnp.sum(residual[:, None] * activated.astype(jnp.float32), 0))
        pair_grad = jnp.dot(lin_grad, pair_w1.T, preferred_element_type=jnp.float32)
        victim_grad = pair_grad[:, :F]
        partner_grad = lax.optimization_barrier(pair_grad[:, F:].astype(jnp.bfloat16))
        dnets_all = dnets_all.at[device, local_blocks[device].reshape(-1)].add(victim_grad)
        dnets_all = dnets_all.at[owners[:, None], remote_blocks[device]].add(partner_grad.astype(jnp.float32).reshape(regions, CAP, F))
        return ((dnets_all, grad_w1, grad_w2, sq_total + jnp.sum(errors * errors)), None)
    start = (jnp.zeros((devices, NET_DEV, F), jnp.float32), jnp.zeros((2 * F, HID), jnp.float32), jnp.zeros((HID,), jnp.float32), jnp.zeros((), jnp.float32))
    (dnets_all, grad_w1, grad_w2, sq_total), _ = lax.scan(pair_step, start, device_ids)

    def layer_step(carry, device):
        dembeds_all, grad_gnn = carry
        joined, pre = layer_inputs(device)
        pre_grad = (dnets_all[device] * gelu_slope(pre)).astype(jnp.bfloat16)
        grad_gnn = grad_gnn + jnp.dot(joined.T, pre_grad, preferred_element_type=jnp.float32)
        cat_grad = jnp.dot(pre_grad, gnn_weight.T, preferred_element_type=jnp.float32)
        agg_grad = lax.optimization_barrier((cat_grad[:, F:] / DEG).astype(jnp.bfloat16)).astype(jnp.float32)
        table_grad = jnp.zeros((NET_DEV + doms * HALO, F), jnp.float32)
        for column in range(DEG):
            table_grad = table_grad.at[neigh_blocks[device][:, column]].add(agg_grad)
        senders, lists = lists_for(device)
        dembeds_all = dembeds_all.at[device].add(dnets_all[device] + cat_grad[:, :F] + table_grad[:NET_DEV])
        returned = lax.optimization_barrier(table_grad[NET_DEV:].astype(jnp.bfloat16))
        dembeds_all = dembeds_all.at[senders[:, None], lists].add(returned.astype(jnp.float32).reshape(doms, HALO, F))
        return ((dembeds_all, grad_gnn), None)
    (dembeds_all, grad_gnn), _ = lax.scan(layer_step, (jnp.zeros((devices, NET_DEV, F), jnp.float32), jnp.zeros((2 * F, F), jnp.float32)), device_ids)
    total_count = jnp.sum(pair_count).astype(jnp.float32)
    root_count = jnp.sqrt(total_count)
    embeds_grad = (dembeds_all * (8.0 * NETS / total_count)).astype(jnp.bfloat16).reshape(NETS, F)
    return (embeds_grad, 8.0 * grad_gnn / root_count, 8.0 * grad_w1 / root_count, 8.0 * grad_w2 / root_count, sq_total / total_count)
```

```python
import functools
import jax
import jax.numpy as jnp
from jax import lax
from jax.sharding import PartitionSpec as P
from jax.experimental import pallas as pl
from jax.experimental.pallas import tpu as pltpu

f32 = jnp.float32
bf16 = jnp.bfloat16
gelu_coef = 0.7978845608
contract_rows = (((0,), (0,)), ((), ()))
contract_cols = (((1,), (1,)), ((), ()))
VMEM_LIMIT = 60 * 1024 * 1024
FIELDS = 8


def gelu_both(value):
    inner = jnp.tanh(gelu_coef * (value + 0.044715 * value * value * value))
    half = 0.5 * (1.0 + inner)
    slope = half + 0.5 * value * (1.0 - inner * inner) * gelu_coef * (
        1.0 + 3.0 * 0.044715 * value * value
    )
    return value * half, slope


def gelu_slope(value):
    return gelu_both(value)[1]


def dot(a, b):
    return jnp.dot(a, b, preferred_element_type=f32)


def call(body, outs, grid, in_specs, out_specs, scratch=(), flops=0, nbytes=0, name=None):
    return pl.pallas_call(
        body,
        out_shape=outs,
        grid=grid,
        in_specs=in_specs,
        out_specs=out_specs,
        scratch_shapes=list(scratch),
        name=name,
        cost_estimate=pl.CostEstimate(flops=flops, bytes_accessed=nbytes, transcendentals=0),
        compiler_params=pltpu.CompilerParams(
            dimension_semantics=("arbitrary",) * len(grid), vmem_limit_bytes=VMEM_LIMIT
        ),
    )


def whole(shape):
    zero = (0,) * len(shape)
    return pl.BlockSpec(shape, lambda *_: zero)


def field_scale(field):
    return -(16.0 ** -field) if field == FIELDS - 1 else 16.0 ** -field


def field_mask(field):
    mask = 15 << (4 * field)
    return mask - (1 << 32) if mask >= (1 << 31) else mask


def expand(words, field):
    return (words & field_mask(field)).astype(f32).astype(bf16)


def agg_own_body(nb_ref, table_ref, words_ref, sum_ref, scaled):
    width = words_ref.shape[1]
    half = FIELDS // 2

    @pl.when(pl.program_id(0) == 0)
    def _():
        for field in range(half):
            scaled[field * width:(field + 1) * width, :] = (
                table_ref[field * width:(field + 1) * width, :].astype(f32) * field_scale(field)
            ).astype(bf16)

    nb = nb_ref[...]
    low = nb & (width - 1)
    shift = 4 * (nb >> (width.bit_length() - 1))
    weight = jnp.where(shift == 4 * (FIELDS - 1), -(1 << 28), jnp.left_shift(1, shift))
    lane = lax.broadcasted_iota(jnp.int32, (nb.shape[0], width), 1)
    words = jnp.zeros((nb.shape[0], width), jnp.int32)
    for d in range(nb.shape[1]):
        words = words + jnp.where(lane == low[:, d:d + 1], weight[:, d:d + 1], 0)
    words_ref[...] = words
    acc = jnp.zeros(sum_ref.shape, f32)
    for field in range(half):
        acc = acc + dot(expand(words, field), scaled[field * width:(field + 1) * width, :])
    sum_ref[...] = acc


def agg_own(neighbours, embeds, tile=256):
    n, degree = neighbours.shape
    f = embeds.shape[1]
    width = 2 * n // FIELDS
    return call(
        agg_own_body,
        (jax.ShapeDtypeStruct((n, width), jnp.int32), jax.ShapeDtypeStruct((n, f), f32)),
        (n // tile,),
        [pl.BlockSpec((tile, degree), lambda i: (i, 0)), whole((n, f))],
        (pl.BlockSpec((tile, width), lambda i: (i, 0)), pl.BlockSpec((tile, f), lambda i: (i, 0))),
        [pltpu.VMEM((n, f), bf16)],
        flops=2 * n * n * f * 4, nbytes=n * width * 4 + n * f * 8, name="agg_own",
    )(neighbours, embeds)


def nets_body(words_ref, sum_ref, recv_ref, emb_ref, gw_ref, pre_ref, agg_ref, nets_ref, scaled):
    width = words_ref.shape[1]
    half = FIELDS // 2
    f = emb_ref.shape[1]

    @pl.when(pl.program_id(0) == 0)
    def _():
        for field in range(half):
            scaled[field * width:(field + 1) * width, :] = (
                recv_ref[field * width:(field + 1) * width, :].astype(f32)
                * field_scale(field + half)
            ).astype(bf16)

    words = words_ref[...]
    acc = sum_ref[...]
    for field in range(half):
        acc = acc + dot(expand(words, field + half), scaled[field * width:(field + 1) * width, :])
    agg = (acc * 0.125).astype(bf16)
    emb = emb_ref[...]
    pre = dot(emb, gw_ref[:f, :]) + dot(agg, gw_ref[f:, :])
    pre_ref[...] = pre
    agg_ref[...] = agg
    nets_ref[...] = (emb.astype(f32) + gelu_both(pre)[0]).astype(bf16)


def make_nets(words, own_sum, received, embeds, gnn_weight, tile=256):
    n, f = embeds.shape
    width = words.shape[1]
    row = lambda i: (i, 0)
    return call(
        nets_body,
        (
            jax.ShapeDtypeStruct((n, f), f32),
            jax.ShapeDtypeStruct((n, f), bf16),
            jax.ShapeDtypeStruct((n, f), bf16),
        ),
        (n // tile,),
        [
            pl.BlockSpec((tile, width), row), pl.BlockSpec((tile, f), row), whole((n, f)),
            pl.BlockSpec((tile, f), row), whole(gnn_weight.shape),
        ],
        tuple(pl.BlockSpec((tile, f), row) for _ in range(3)),
        [pltpu.VMEM((n, f), bf16)],
        flops=2 * n * n * f * 4, nbytes=n * width * 4 + n * f * 16, name="make_nets",
    )(words, own_sum, received, embeds, gnn_weight)


def column(ids_ref, q):
    return ids_ref[...].T[:, q:q + 1]


def one_hot(ids, n):
    return (ids == lax.broadcasted_iota(jnp.int32, (ids.shape[0], n), 1)).astype(f32).astype(bf16)


def pick(ids_all, q, count):
    lane = lax.broadcasted_iota(jnp.int32, ids_all.shape, 1)
    return jnp.sum(jnp.where(lane == q, ids_all, 0), axis=1, keepdims=True)


def gather_body(ids_ref, table_ref, out_ref):
    ids = ids_ref[0].T
    out_ref[0] = dot(one_hot(ids, table_ref.shape[0]), table_ref[...]).astype(bf16)


def gather_rows(ids, table):
    groups, count = ids.shape
    n, f = table.shape
    return call(
        gather_body,
        jax.ShapeDtypeStruct((groups, count, f), bf16),
        (groups,),
        [pl.BlockSpec((1, 1, count), lambda i: (i, 0, 0)), whole((n, f))],
        pl.BlockSpec((1, count, f), lambda i: (i, 0, 0)),
        flops=2 * groups * count * n * f, nbytes=groups * count * f * 2, name="gather_rows",
    )(ids.reshape(groups, 1, count), table)


def victim_body(ids_ref, table_ref, w_ref, out_ref):
    ids = ids_ref[0].T
    rows = dot(one_hot(ids, table_ref.shape[0]), table_ref[...]).astype(bf16)
    out_ref[0] = dot(rows, w_ref[...])


def victim_part(ids, table, w1a):
    groups, count = ids.shape
    n, f = table.shape
    return call(
        victim_body,
        jax.ShapeDtypeStruct((groups, count, w1a.shape[1]), f32),
        (groups,),
        [pl.BlockSpec((1, 1, count), lambda i: (i, 0, 0)), whole((n, f)), whole(w1a.shape)],
        pl.BlockSpec((1, count, w1a.shape[1]), lambda i: (i, 0, 0)),
        flops=2 * groups * count * (n + f) * f, nbytes=groups * count * f * 4, name="victim_part",
    )(ids.reshape(groups, 1, count), table, w1a)


def pair_body(part_ref, va_ref, w1b_ref, w2m_ref, w2_ref, tgt_ref, cnt_ref, grad_ref, w2g_ref, sq_ref):
    q = pl.program_id(0)
    linear = va_ref[0] + dot(part_ref[0], w1b_ref[...])
    act, slope = gelu_both(linear)
    act = act.astype(bf16)
    scores = dot(act, w2m_ref[...])
    count = scores.shape[0]
    target = tgt_ref[0].T
    live = lax.broadcasted_iota(jnp.int32, (count, 1), 0) < cnt_ref[0, q]
    errors = jnp.where(live, scores - target, 0.0)
    residual = 2.0 * errors
    grad_ref[0] = (residual * w2_ref[...].astype(f32) * slope).astype(bf16)

    @pl.when(q == 0)
    def _():
        w2g_ref[...] = jnp.zeros_like(w2g_ref)
        sq_ref[...] = jnp.zeros_like(sq_ref)

    w2g_ref[...] += jnp.sum(residual * act.astype(f32), axis=0, keepdims=True)
    sq_ref[...] += jnp.sum(errors * errors, axis=0, keepdims=True)


def pair_step(partner, va, w1b, w2, targets, counts):
    groups, count, f = partner.shape
    h = w1b.shape[1]
    block = lambda i: (i, 0, 0)
    return call(
        pair_body,
        (
            jax.ShapeDtypeStruct((groups, count, h), bf16),
            jax.ShapeDtypeStruct((1, h), f32),
            jax.ShapeDtypeStruct((1, h), f32),
        ),
        (groups,),
        [
            pl.BlockSpec((1, count, f), block), pl.BlockSpec((1, count, h), block),
            whole((f, h)), whole((h, h)), whole((1, h)),
            pl.BlockSpec((1, 1, count), block), pl.BlockSpec(memory_space=pltpu.SMEM),
        ],
        (pl.BlockSpec((1, count, h), block), whole((1, h)), whole((1, h))),
        flops=2 * groups * count * 2 * f * h, nbytes=groups * count * h * 8, name="pair_step",
    )(
        partner, va, w1b, jnp.broadcast_to(w2[:, None], (h, h)), w2[None, :],
        targets.reshape(groups, 1, count), counts,
    )


def split(value):
    high = value.astype(bf16)
    return high, (value - high.astype(f32)).astype(bf16)


def scatter_loop(ids_ref, grad_ref, acc, tile):
    groups, count, f = grad_ref.shape
    n = acc.shape[0]

    def step(i, _):
        base = pl.multiple_of(i * tile, tile)
        row = lax.broadcasted_iota(jnp.int32, (tile, count), 0) + base
        total = jnp.zeros((tile, f), f32)
        for q in range(groups):
            hot = (row == ids_ref[q:q + 1, :]).astype(f32).astype(bf16)
            total = total + dot(hot, grad_ref[q])
        acc[pl.ds(base, tile), :] = total
        return 0

    lax.fori_loop(0, n // tile, step, 0)


def scatter_victim_body(ids_ref, grad_ref, nets_ref, w_ref, ng_ref, wg_ref, acc):
    scatter_loop(ids_ref, grad_ref, acc, 256)
    high, low = split(acc[...])
    ng_ref[...] = lax.dot_general(high, w_ref[...], contract_cols, preferred_element_type=f32) + lax.dot_general(low, w_ref[...], contract_cols, preferred_element_type=f32)
    nets = nets_ref[...]
    wg_ref[...] = lax.dot_general(nets, high, contract_rows, preferred_element_type=f32) + lax.dot_general(nets, low, contract_rows, preferred_element_type=f32)


def scatter_victim(ids, grad, nets, w1a):
    n, f = nets.shape
    h = w1a.shape[1]
    groups, count, _ = grad.shape
    return call(
        scatter_victim_body,
        (jax.ShapeDtypeStruct((n, f), f32), jax.ShapeDtypeStruct((f, h), f32)),
        (1,),
        [whole(ids.shape), whole(grad.shape), whole(nets.shape), whole(w1a.shape)],
        (whole((n, f)), whole((f, h))),
        [pltpu.VMEM((n, h), f32)],
        flops=2 * groups * count * n * h, nbytes=groups * count * h * 2 + n * f * 6, name="scatter_victim",
    )(ids, grad, nets, w1a)


def back_body(ids_ref, grad_ref, nets_ref, w_ref, ngv_ref, pre_ref, emb_ref, agg_ref, gw_ref, wg_ref, gg_ref, base_ref, ag_ref, acc):
    scatter_loop(ids_ref, grad_ref, acc, 256)
    f = emb_ref.shape[1]
    tile = 256

    def step(i, _):
        rows = pl.ds(pl.multiple_of(i * tile, tile), tile)
        high, low = split(acc[rows, :])
        w = w_ref[...]
        ng = ngv_ref[rows, :] + lax.dot_general(high, w, contract_cols, preferred_element_type=f32) + lax.dot_general(low, w, contract_cols, preferred_element_type=f32)
        pg = (ng * gelu_slope(pre_ref[rows, :])).astype(bf16)
        cat_own = lax.dot_general(pg, gw_ref[:f, :], contract_cols, preferred_element_type=f32)
        cat_agg = lax.dot_general(pg, gw_ref[f:, :], contract_cols, preferred_element_type=f32)
        base_ref[rows, :] = ng + cat_own
        ag_ref[rows, :] = (cat_agg * 0.125).astype(bf16)
        nets = nets_ref[rows, :]
        wg = lax.dot_general(nets, high, contract_rows, preferred_element_type=f32) + lax.dot_general(nets, low, contract_rows, preferred_element_type=f32)
        g1 = lax.dot_general(emb_ref[rows, :], pg, contract_rows, preferred_element_type=f32)
        g2 = lax.dot_general(agg_ref[rows, :], pg, contract_rows, preferred_element_type=f32)
        wg_ref[...] += wg
        gg_ref[:f, :] += g1
        gg_ref[f:, :] += g2
        return 0

    wg_ref[...] = jnp.zeros_like(wg_ref)
    gg_ref[...] = jnp.zeros_like(gg_ref)
    lax.fori_loop(0, acc.shape[0] // tile, step, 0)


def back(ids, grad, nets, w1b, ngv, pre, embeds, aggregate, gnn_weight):
    n, f = nets.shape
    h = w1b.shape[1]
    groups, count, _ = grad.shape
    args = (ids, grad, nets, w1b, ngv, pre, embeds, aggregate, gnn_weight)
    return call(
        back_body,
        (
            jax.ShapeDtypeStruct((f, h), f32), jax.ShapeDtypeStruct((2 * f, f), f32),
            jax.ShapeDtypeStruct((n, f), f32), jax.ShapeDtypeStruct((n, f), bf16),
        ),
        (1,),
        [whole(a.shape) for a in args],
        (whole((f, h)), whole((2 * f, f)), whole((n, f)), whole((n, f))),
        [pltpu.VMEM((n, h), f32)],
        flops=2 * groups * count * n * h, nbytes=groups * count * h * 2 + n * f * 20, name="back",
    )(*args)


def table_body(first, words_ref, ag_ref, out_ref):
    for j in range(FIELDS // 2):
        hot = expand(words_ref[...], first + j)
        part = lax.dot_general(hot, ag_ref[...], contract_rows, preferred_element_type=f32)
        out_ref[j] = (part * field_scale(first + j)).astype(out_ref.dtype)


def table_back(words, ag, first, dtype, name, tile=256):
    n, width = words.shape
    f = ag.shape[1]
    half = FIELDS // 2
    out = call(
        functools.partial(table_body, first),
        jax.ShapeDtypeStruct((half, width, f), dtype),
        (width // tile,),
        [pl.BlockSpec((n, tile), lambda i: (0, i)), whole((n, f))],
        pl.BlockSpec((half, tile, f), lambda i: (0, i, 0)),
        flops=2 * n * n * f * 2, nbytes=n * width * 4 + n * f * 6, name=name,
    )(words, ag)
    return out.reshape(half * width, f)


def final_body(ids_ref, ret_ref, base_ref, own_ref, scale_ref, out_ref):
    tile, f = out_ref.shape
    peers, halo = ids_ref.shape
    row = lax.broadcasted_iota(jnp.int32, (tile, halo), 0) + pl.program_id(0) * tile
    total = base_ref[...] + own_ref[...]
    for p in range(peers):
        hot = (row == ids_ref[p:p + 1, :]).astype(f32).astype(bf16)
        total = total + dot(hot, ret_ref[p])
    out_ref[...] = (total * scale_ref[0]).astype(bf16)


def final(ids, returned, base, own, scale, tile=256):
    n, f = base.shape
    row = lambda i: (i, 0)
    return call(
        final_body,
        jax.ShapeDtypeStruct((n, f), bf16),
        (n // tile,),
        [
            whole(ids.shape), whole(returned.shape), pl.BlockSpec((tile, f), row),
            pl.BlockSpec((tile, f), row), pl.BlockSpec(memory_space=pltpu.SMEM),
        ],
        pl.BlockSpec((tile, f), row),
        flops=2 * n * n * f, nbytes=n * f * 12, name="final",
    )(ids, returned, base, own, scale)
MESH = pl.DeviceIdType.MESH


def reduce_body(n_chip, n_dom, x_ref, out_ref, r0, s0, r1, s1, r2, s2, e0, ea, e1, eb, e2,
                send0, recv0, send1, recv1, send2, recv2, gsend0, grecv0, gsend1, grecv1, gsend2, grecv2,
                es0, er0, es1, er1, es2, er2):
    region = lax.axis_index("region")
    dom = lax.axis_index("dom")
    core = lax.rem(region, 2)
    chip = region // 2
    rows = out_ref.shape[0] - 8
    q0 = rows // 2
    q1 = q0 // n_chip
    q2 = q1 // n_dom

    def at(r, d):
        return (r, d)

    pair = at(chip * 2 + 1 - core, dom)
    chips = [at(lax.rem(chip + k, n_chip) * 2 + core, dom) for k in range(1, n_chip)]
    doms = [at(region, lax.rem(dom + k, n_dom)) for k in range(1, n_dom)]
    barrier = pltpu.get_barrier_semaphore()
    for device in [pair] + chips + doms:
        pl.semaphore_signal(barrier, inc=1, device_id=device, device_id_type=MESH)
    pl.semaphore_wait(barrier, 1 + len(chips) + len(doms))

    def send(src, dst, ssem, rsem, device):
        copy = pltpu.make_async_remote_copy(src_ref=src, dst_ref=dst, send_sem=ssem, recv_sem=rsem,
                                            device_id=device, device_id_type=MESH)
        copy.start()
        return copy

    c0 = send(x_ref.at[pl.ds((1 - core) * q0, q0)], r0, send0, recv0, pair)
    c0e = send(x_ref.at[pl.ds(rows, 8)], e0, es0, er0, pair)
    c0.wait()
    c0e.wait()
    s0[...] = x_ref[pl.ds(core * q0, q0), :] + r0[...]
    ea[...] = x_ref[pl.ds(rows, 8), :] + e0[...]
    copies = []
    for k in range(1, n_chip):
        peer = lax.rem(chip + k, n_chip)
        copies.append(send(s0.at[pl.ds(peer * q1, q1)], r1.at[k - 1], send1.at[k - 1], recv1.at[k - 1], chips[k - 1]))
        copies.append(send(ea, e1.at[k - 1], es1.at[k - 1], er1.at[k - 1], chips[k - 1]))
    for copy in copies:
        copy.wait()
    total = s0[pl.ds(chip * q1, q1), :]
    etotal = ea[...]
    for k in range(1, n_chip):
        total = total + r1[k - 1]
        etotal = etotal + e1[k - 1]
    s1[...] = total
    eb[...] = etotal
    copies = []
    for k in range(1, n_dom):
        peer = lax.rem(dom + k, n_dom)
        copies.append(send(s1.at[pl.ds(peer * q2, q2)], r2.at[k - 1], send2.at[k - 1], recv2.at[k - 1], doms[k - 1]))
        copies.append(send(eb, e2.at[k - 1], es2.at[k - 1], er2.at[k - 1], doms[k - 1]))
    for copy in copies:
        copy.wait()
    total = s1[pl.ds(dom * q2, q2), :]
    etotal = eb[...]
    for k in range(1, n_dom):
        total = total + r2[k - 1]
        etotal = etotal + e2[k - 1]
    mine = core * q0 + chip * q1 + dom * q2
    out_ref[pl.ds(mine, q2), :] = total
    out_ref[pl.ds(rows, 8), :] = etotal
    block = out_ref.at[pl.ds(mine, q2)]
    copies = [send(block, block, gsend2.at[k - 1], grecv2.at[k - 1], doms[k - 1]) for k in range(1, n_dom)]
    for copy in copies:
        copy.wait()
    block = out_ref.at[pl.ds(core * q0 + chip * q1, q1)]
    copies = [send(block, block, gsend1.at[k - 1], grecv1.at[k - 1], chips[k - 1]) for k in range(1, n_chip)]
    for copy in copies:
        copy.wait()
    block = out_ref.at[pl.ds(core * q0, q0)]
    send(block, block, gsend0, grecv0, pair).wait()


def reduce_all(x, n_region, n_dom):
    rows = x.shape[0] - 8
    f = x.shape[1]
    n_chip = n_region // 2
    q0 = rows // 2
    q1 = q0 // n_chip
    q2 = q1 // n_dom
    dma = pltpu.SemaphoreType.DMA
    vm = lambda *shape: pltpu.VMEM(shape, f32)
    return pl.pallas_call(
        functools.partial(reduce_body, n_chip, n_dom),
        out_shape=jax.ShapeDtypeStruct(x.shape, f32),
        in_specs=[pl.BlockSpec(memory_space=pltpu.VMEM)],
        out_specs=pl.BlockSpec(memory_space=pltpu.VMEM),
        scratch_shapes=[
            vm(q0, f), vm(q0, f), vm(n_chip - 1, q1, f), vm(q1, f), vm(n_dom - 1, q2, f), vm(q2, f),
            vm(8, f), vm(8, f), vm(n_chip - 1, 8, f), vm(8, f), vm(n_dom - 1, 8, f),
            dma, dma, dma((n_chip - 1,)), dma((n_chip - 1,)), dma((n_dom - 1,)), dma((n_dom - 1,)),
            dma, dma, dma((n_chip - 1,)), dma((n_chip - 1,)), dma((n_dom - 1,)), dma((n_dom - 1,)),
            dma, dma, dma((n_chip - 1,)), dma((n_chip - 1,)), dma((n_dom - 1,)), dma((n_dom - 1,)),
        ],
        name="reduce_all",
        compiler_params=pltpu.CompilerParams(collective_id=0, has_side_effects=True, vmem_limit_bytes=VMEM_LIMIT),
    )(x)
def local(
    embeds, neighbours, halo_send, gnn_weight, pair_local, pair_remote, pair_count, targets, pair_w1, pair_w2
):
    n, f = embeds.shape
    peers, halo = halo_send.shape
    regions, slots = pair_local.shape
    n_region, n_dom = lax.axis_size("region"), lax.axis_size("dom")
    nets_total = n * n_region * n_dom
    w1a, w1b = pair_w1[:f], pair_w1[f:]
    exchange = functools.partial(lax.all_to_all, split_axis=0, concat_axis=0, tiled=True)

    outgoing = gather_rows(halo_send.reshape(4, -1), embeds).reshape(peers, halo, f)
    received = exchange(outgoing, "dom").reshape(-1, f)
    asked = exchange(pair_remote, "region")
    words, own_sum = agg_own(neighbours, embeds)
    pre, aggregate, nets = make_nets(words, own_sum, received, embeds, gnn_weight)
    partner = exchange(gather_rows(asked, nets), "region")
    va = victim_part(pair_local, nets, w1a)
    lin_grad, w2_grad, sq = pair_step(partner, va, w1b, pair_w2, targets, pair_count)
    returned = exchange(lin_grad, "region")
    ng_victim, w1a_grad = scatter_victim(pair_local, lin_grad, nets, w1a)
    w1b_grad, gnn_grad, base, agg_grad = back(
        asked, returned, nets, w1b, ng_victim, pre, embeds, aggregate, gnn_weight
    )
    halo_back = table_back(words, agg_grad, FIELDS // 2, bf16, "halo_back").reshape(peers, halo, f)
    returned_halo = exchange(halo_back, "dom")
    own = table_back(words, agg_grad, 0, f32, "own_back")
    extra = jnp.concatenate(
        [
            w2_grad, sq,
            jnp.broadcast_to(jnp.sum(pair_count).astype(f32), (1, f)),
            jnp.zeros((5, f), f32),
        ],
        0,
    )
    sums = reduce_all(jnp.concatenate([gnn_grad, w1a_grad, w1b_grad, extra], 0), n_region, n_dom)
    total = sums[4 * f + 2, 0]
    root = 8.0 / jnp.sqrt(total)
    scale = (8.0 * nets_total / total).reshape(1)
    embeds_grad = final(halo_send, returned_halo, base, own, scale)
    return (
        embeds_grad,
        sums[: 2 * f] * root,
        sums[2 * f : 4 * f] * root,
        sums[4 * f] * root,
        sums[4 * f + 1, 0] / total,
    )


def solution(mesh):
    both = P(("region", "dom"), None)
    in_specs = (both, both, both, P(), both, both, both, both, P(), P())
    out_specs = (both, P(), P(), P(), P())
    return jax.shard_map(local, mesh=mesh, in_specs=in_specs, out_specs=out_specs, check_vma=False)
```

```python
import functools
import jax
import jax.numpy as jnp
from jax import lax
from jax.experimental import pallas as pl
from jax.experimental.pallas import tpu as pltpu
from jax.sharding import PartitionSpec as P

f32 = jnp.float32
bf16 = jnp.bfloat16
gelu_coef = 0.7978845608
contract_rows = (((0,), (0,)), ((), ()))
contract_cols = (((1,), (1,)), ((), ()))
VMEM_LIMIT = 62 * 1024 * 1024
MESH = pl.DeviceIdType.MESH
FIELDS = 8
HALF = FIELDS // 2


def gelu_both(value):
    inner = jnp.tanh(gelu_coef * (value + 0.044715 * value * value * value))
    half = 0.5 * (1.0 + inner)
    slope = half + 0.5 * value * (1.0 - inner * inner) * gelu_coef * (
        1.0 + 3.0 * 0.044715 * value * value
    )
    return value * half, slope


def dot(a, b):
    return jnp.dot(a, b, preferred_element_type=f32)


def dot_rows(a, b):
    return lax.dot_general(a, b, contract_rows, preferred_element_type=f32)


def dot_cols(a, b):
    return lax.dot_general(a, b, contract_cols, preferred_element_type=f32)


def split(value):
    high = value.astype(bf16)
    return high, (value - high.astype(f32)).astype(bf16)


def rows_at(i, tile):
    return pl.ds(pl.multiple_of(i * tile, tile), tile)


def lane_hot(ids, n):
    return (ids == lax.broadcasted_iota(jnp.int32, (ids.shape[0], n), 1)).astype(f32).astype(bf16)


def row_hot(base, tile, ids):
    row = lax.broadcasted_iota(jnp.int32, (tile, ids.shape[1]), 0)
    return (row == ids - base).astype(f32).astype(bf16)


def counts_of(words, field):
    return ((words >> (4 * field)) & 15).astype(f32).astype(bf16)


class Place:
    def __init__(self, n_region, n_dom):
        self.n_region, self.n_dom = n_region, n_dom
        self.n_chip = n_region // 2
        self.per = n_dom // HALF
        self.region = lax.axis_index("region")
        self.dom = lax.axis_index("dom")
        self.chip = self.region // 2
        self.core = lax.rem(self.region, 2)

    def region_to(self, m):
        chip = lax.rem(self.chip + lax.rem(m, self.n_chip), self.n_chip)
        return chip * 2 + lax.rem(self.core + m // self.n_chip, 2)

    def region_from(self, m):
        chip = lax.rem(self.chip + self.n_chip - lax.rem(m, self.n_chip), self.n_chip)
        return chip * 2 + lax.rem(self.core + m // self.n_chip, 2)

    def field_to(self, i):
        return lax.rem(self.dom // self.per + i, HALF)

    def sub_to(self, j):
        return lax.rem(lax.rem(self.dom, self.per) + j, self.per)

    def dom_to(self, k):
        return lax.rem(self.dom + k, self.n_dom)

    def at_region(self, r):
        return (r, self.dom)

    def at_dom(self, d):
        return (self.region, d)


def remote(src, dst, ssem, rsem, device):
    return pltpu.make_async_remote_copy(
        src_ref=src, dst_ref=dst, send_sem=ssem, recv_sem=rsem, device_id=device, device_id_type=MESH
    )


def greet(devices):
    barrier = pltpu.get_barrier_semaphore()
    for device in devices:
        pl.semaphore_signal(barrier, inc=1, device_id=device, device_id_type=MESH)
    pl.semaphore_wait(barrier, len(devices))


def vmem():
    return pl.BlockSpec(memory_space=pltpu.VMEM)


def smem():
    return pl.BlockSpec(memory_space=pltpu.SMEM)


def kernel_call(body, outs, in_specs, scratch, collective, name, out_specs=None):
    single = not isinstance(outs, tuple)
    specs = vmem() if single else tuple(vmem() for _ in outs)
    params = dict(vmem_limit_bytes=VMEM_LIMIT)
    if collective is not None:
        params.update(collective_id=collective, has_side_effects=True)
    return pl.pallas_call(
        body, out_shape=outs, in_specs=in_specs, out_specs=specs, scratch_shapes=scratch, name=name,
        compiler_params=pltpu.CompilerParams(**params),
    )


def head_body(n_region, n_dom, emb, nb, hs, pr, gw, words, pre, agg, nets, asked,
              outgoing, recv, sums, hsend, hrecv, asend, arecv):
    place = Place(n_region, n_dom)
    per = place.per
    n, f = emb.shape
    halo = hs.shape[1]
    greet([place.at_dom(place.dom_to(k)) for k in range(1, n_dom)]
          + [place.at_region(place.region_to(m)) for m in range(1, n_region)])

    def ask(m):
        r = place.region_to(m)
        return remote(pr.at[pl.ds(r, 1)], asked.at[pl.ds(place.region, 1)],
                      asend.at[m], arecv.at[m], place.at_region(r))

    def halo_copy(i, j):
        field, sub = place.field_to(i), place.sub_to(j)
        return remote(outgoing.at[field * per + sub], recv.at[place.dom],
                      hsend.at[i * per + j], hrecv.at[i * per + j], place.at_dom(field * per + sub))

    for m in range(1, n_region):
        ask(m).start()
    asked[pl.ds(place.region, 1), :] = pr[pl.ds(place.region, 1), :]

    for i in range(HALF):
        field = place.field_to(i)
        ids = jnp.concatenate([hs[pl.ds(field * per + s, 1), :] for s in range(per)], 1).T
        rows = dot(lane_hot(ids, n), emb[...]).astype(bf16)
        for s in range(per):
            outgoing[field * per + s] = rows[s * halo:(s + 1) * halo]
        for j in range(per):
            if i or j:
                halo_copy(i, j).start()
    recv[place.dom] = outgoing[place.dom]

    tile = 256
    width = words.shape[1]
    wbits = width.bit_length() - 1

    def own_step(t, _):
        rows = rows_at(t, tile)
        ids = nb[:, rows].T
        low = ids & (width - 1)
        weight = jnp.left_shift(1, 4 * (ids >> wbits))
        lane = lax.broadcasted_iota(jnp.int32, (tile, width), 1)
        word = jnp.zeros((tile, width), jnp.int32)
        for d in range(ids.shape[1]):
            word = word + jnp.where(lane == low[:, d:d + 1], weight[:, d:d + 1], 0)
        words[rows, :] = word
        acc = jnp.zeros((tile, f), f32)
        for field in range(HALF):
            acc = acc + dot(counts_of(word, field), emb[field * width:(field + 1) * width, :])
        sums[rows, :] = acc
        return 0

    lax.fori_loop(0, n // tile, own_step, 0)
    for i in range(HALF):
        for j in range(per):
            if i or j:
                halo_copy(i, j).wait()

    def halo_step(t, _):
        rows = rows_at(t, tile)
        word = words[rows, :]
        acc = sums[rows, :]
        for field in range(HALF):
            table = recv[field * per:(field + 1) * per].reshape(width, f)
            acc = acc + dot(counts_of(word, field + HALF), table)
        mean = (acc * 0.125).astype(bf16)
        own = emb[rows, :]
        lin = dot(own, gw[:f, :]) + dot(mean, gw[f:, :])
        pre[rows, :] = lin
        agg[rows, :] = mean
        nets[rows, :] = (own.astype(f32) + gelu_both(lin)[0]).astype(bf16)
        return 0

    lax.fori_loop(0, n // tile, halo_step, 0)
    for m in range(1, n_region):
        ask(m).wait()


def head(n_region, n_dom, embeds, neighbours, halo_send, pair_remote, gnn_weight):
    n, f = embeds.shape
    peers, halo = halo_send.shape
    width = 2 * n // FIELDS
    dma = pltpu.SemaphoreType.DMA
    shape = jax.ShapeDtypeStruct
    return kernel_call(
        functools.partial(head_body, n_region, n_dom),
        (
            shape((n, width), jnp.int32), shape((n, f), f32), shape((n, f), bf16), shape((n, f), bf16),
            shape(pair_remote.shape, jnp.int32),
        ),
        [vmem()] * 5,
        [
            pltpu.VMEM((peers, halo, f), bf16), pltpu.VMEM((peers, halo, f), bf16), pltpu.VMEM((n, f), f32),
            dma((n_dom,)), dma((n_dom,)), dma((n_region,)), dma((n_region,)),
        ],
        1, "head",
    )(embeds, neighbours.T, halo_send, pair_remote, gnn_weight)


def pair_body(n_region, n_dom, nets, asked, loc, tgt, cnt, w1, w2, sv, sp, small,
              outgoing, partner, grad, back, va, fsend, frecv, bsend, brecv):
    place = Place(n_region, n_dom)
    me = place.region
    n, f = nets.shape
    count = loc.shape[1]
    h = w1.shape[1]
    greet([place.at_region(place.region_to(m)) for m in range(1, n_region)])

    def out_copy(m):
        r = place.region_to(m)
        return remote(outgoing.at[r], partner.at[me], fsend.at[m], frecv.at[m], place.at_region(r))

    def back_copy(m):
        r = place.region_from(m)
        return remote(grad.at[r], back.at[me], bsend.at[m], brecv.at[m], place.at_region(r))

    def fetch(ids_ref, r):
        ids = ids_ref[pl.ds(r, 1), :].T
        return dot(lane_hot(ids, n), nets[...]).astype(bf16)

    def gather_step(m, _):
        outgoing[place.region_to(m)] = fetch(asked, place.region_to(m))
        out_copy(m).start()
        return 0

    lax.fori_loop(1, n_region, gather_step, 0)
    partner[me] = fetch(asked, me)

    def victim_step(q, _):
        va[q] = dot(fetch(loc, q), w1[:f, :])
        return 0

    lax.fori_loop(0, n_region, victim_step, 0)
    w2row = w2[...]
    w2mat = jnp.broadcast_to(w2row.astype(f32), (h, h)).T.astype(bf16)
    w2f = w2row.astype(f32)

    def pair_step(m):
        q = place.region_from(m)
        linear = va[q] + dot(partner[q], w1[f:, :])
        act, slope = gelu_both(linear)
        act = act.astype(bf16)
        scores = dot(act, w2mat)
        target = tgt[pl.ds(q, 1), :].T
        live = lax.broadcasted_iota(jnp.int32, (count, 1), 0) < cnt[0, q]
        errors = jnp.where(live, scores - target, 0.0)
        residual = 2.0 * errors
        grad[q] = (residual * w2f * slope).astype(bf16)
        small[0:1, :] += jnp.sum(residual * act.astype(f32), axis=0, keepdims=True)
        small[1:2, :] += jnp.sum(errors * errors, axis=0, keepdims=True)

    small[...] = jnp.zeros_like(small)
    live_count = cnt[0, 0]
    for q in range(1, n_region):
        live_count = live_count + cnt[0, q]
    small[2:3, :] = jnp.zeros((1, h), f32) + live_count.astype(f32)
    pair_step(0)

    def away_step(m, _):
        out_copy(m).wait_recv()
        pair_step(m)
        back_copy(m).start()
        return 0

    lax.fori_loop(1, n_region, away_step, 0)
    tile = 512

    def victim_scatter(t, _):
        total = jnp.zeros((tile, h), f32)
        for q in range(n_region):
            total = total + dot(row_hot(t * tile, tile, loc[q:q + 1, :]), grad[q])
        sv[rows_at(t, tile), :] = total
        return 0

    lax.fori_loop(0, n // tile, victim_scatter, 0)

    def self_scatter(t, _):
        sp[rows_at(t, tile), :] = dot(row_hot(t * tile, tile, asked[pl.ds(me, 1), :]), grad[me])
        return 0

    lax.fori_loop(0, n // tile, self_scatter, 0)

    def partner_scatter(m, _):
        r = place.region_to(m)
        back_copy(m).wait_recv()
        ids = asked[pl.ds(r, 1), :]
        rows_back = back[r]
        for t in range(n // tile):
            sp[t * tile:(t + 1) * tile, :] += dot(row_hot(t * tile, tile, ids), rows_back)
        return 0

    lax.fori_loop(1, n_region, partner_scatter, 0)

    def drain(m, _):
        out_copy(m).wait_send()
        back_copy(m).wait_send()
        return 0

    lax.fori_loop(1, n_region, drain, 0)


def pair(n_region, n_dom, nets, asked, pair_local, targets, pair_count, pair_w1, pair_w2):
    n, f = nets.shape
    h = pair_w1.shape[1]
    regions, slots = pair_local.shape
    dma = pltpu.SemaphoreType.DMA
    shape = jax.ShapeDtypeStruct
    blocks = pltpu.VMEM((regions, slots, f), bf16)
    return kernel_call(
        functools.partial(pair_body, n_region, n_dom),
        (shape((n, h), f32), shape((n, h), f32), shape((8, h), f32)),
        [vmem()] * 4 + [smem()] + [vmem()] * 2,
        [blocks, blocks, blocks, blocks, pltpu.VMEM((regions, slots, h), f32)] + [dma((n_region,))] * 4,
        2, "pair",
    )(nets, asked, pair_local, targets, pair_count, pair_w1, pair_w2[None, :])


def middle_body(sv, sp, nets, pre, emb, agg, w1, gw, small, base, ag, load):
    n, f = nets.shape
    tile = 256

    load[:4 * f, :] = jnp.zeros((4 * f, f), f32)
    load[4 * f:, :] = small[...]

    def step(t, _):
        rows = rows_at(t, tile)
        vh, vl = split(sv[rows, :])
        ph, plo = split(sp[rows, :])
        ng = dot_cols(vh, w1[:f, :]) + dot_cols(vl, w1[:f, :]) + dot_cols(ph, w1[f:, :]) + dot_cols(plo, w1[f:, :])
        pg = (ng * gelu_both(pre[rows, :])[1]).astype(bf16)
        base[rows, :] = ng + dot_cols(pg, gw[:f, :])
        ag[rows, :] = (dot_cols(pg, gw[f:, :]) * 0.125).astype(bf16)
        own = nets[rows, :]
        load[:f, :] += dot_rows(emb[rows, :], pg)
        load[f:2 * f, :] += dot_rows(agg[rows, :], pg)
        load[2 * f:3 * f, :] += dot_rows(own, vh) + dot_rows(own, vl)
        load[3 * f:4 * f, :] += dot_rows(own, ph) + dot_rows(own, plo)
        return 0

    lax.fori_loop(0, n // tile, step, 0)


def middle(sv, sp, nets, pre, embeds, aggregate, pair_w1, gnn_weight, small):
    n, f = nets.shape
    shape = jax.ShapeDtypeStruct
    return kernel_call(
        middle_body,
        (shape((n, f), f32), shape((n, f), bf16), shape((4 * f + 8, f), f32)),
        [vmem()] * 9, [], None, "middle",
    )(sv, sp, nets, pre, embeds, aggregate, pair_w1, gnn_weight, small)


def tail_body(n_region, n_dom, words, ag, base, hs, load, out, sums, extra,
              outgoing, ret, acc, r0, s0, r1, s1, r2, e0, ea, e1, eb, e2,
              hsend, hrecv, send0, recv0, send1, recv1, send2, recv2,
              gsend0, grecv0, gsend1, grecv1, gsend2, grecv2, es0, er0, es1, er1, es2, er2):
    place = Place(n_region, n_dom)
    n_chip, per = place.n_chip, place.per
    n, f = ag.shape
    halo = hs.shape[1]
    width = words.shape[1]
    rows = sums.shape[0]
    q0 = rows // 2
    q1 = q0 // n_chip
    q2 = q1 // n_dom
    core, chip, dom = place.core, place.chip, place.dom
    twin = place.at_region(chip * 2 + 1 - core)
    chips = [place.at_region(lax.rem(chip + k, n_chip) * 2 + core) for k in range(1, n_chip)]
    doms = [place.at_dom(place.dom_to(k)) for k in range(1, n_dom)]
    greet([twin] + chips + doms)

    c0 = [
        remote(load.at[pl.ds((1 - core) * q0, q0)], r0, send0, recv0, twin),
        remote(load.at[pl.ds(rows, 8)], e0, es0, er0, twin),
    ]
    for copy in c0:
        copy.start()

    def halo_copy(i, j):
        field, sub = place.field_to(i), place.sub_to(j)
        return remote(outgoing.at[field * per + sub], ret.at[dom],
                      hsend.at[i * per + j], hrecv.at[i * per + j], place.at_dom(field * per + sub))

    for i in range(HALF):
        field = place.field_to(i)
        part = dot_rows(counts_of(words[...], field + HALF), ag[...]).astype(bf16)
        for s in range(per):
            outgoing[field * per + s] = part[s * halo:(s + 1) * halo]
        for j in range(per):
            if i or j:
                halo_copy(i, j).start()
    ret[dom] = outgoing[dom]

    def own_field(field):
        part = slice(field * width, (field + 1) * width)
        acc[part, :] = base[part, :] + dot_rows(counts_of(words[...], field), ag[...])

    for copy in c0:
        copy.wait()
    s0[...] = load[pl.ds(core * q0, q0), :] + r0[...]
    ea[...] = load[pl.ds(rows, 8), :] + e0[...]
    c1 = []
    for k in range(1, n_chip):
        peer = lax.rem(chip + k, n_chip)
        c1.append(remote(s0.at[pl.ds(peer * q1, q1)], r1.at[k - 1], send1.at[k - 1], recv1.at[k - 1], chips[k - 1]))
        c1.append(remote(ea, e1.at[k - 1], es1.at[k - 1], er1.at[k - 1], chips[k - 1]))
    for copy in c1:
        copy.start()
    own_field(0)
    own_field(1)
    for copy in c1:
        copy.wait()
    total = s0[pl.ds(chip * q1, q1), :]
    etotal = ea[...]
    for k in range(1, n_chip):
        total = total + r1[k - 1]
        etotal = etotal + e1[k - 1]
    s1[...] = total
    eb[...] = etotal
    c2 = []
    for k in range(1, n_dom):
        peer = place.dom_to(k)
        c2.append(remote(s1.at[pl.ds(peer * q2, q2)], r2.at[k - 1], send2.at[k - 1], recv2.at[k - 1], doms[k - 1]))
        c2.append(remote(eb, e2.at[k - 1], es2.at[k - 1], er2.at[k - 1], doms[k - 1]))
    for copy in c2:
        copy.start()
    own_field(2)
    own_field(3)
    for copy in c2:
        copy.wait()
    total = s1[pl.ds(dom * q2, q2), :]
    etotal = eb[...]
    for k in range(1, n_dom):
        total = total + r2[k - 1]
        etotal = etotal + e2[k - 1]
    live = etotal[2:3, :]
    root = 8.0 / jnp.sqrt(live)
    mine = core * q0 + chip * q1 + dom * q2
    sums[pl.ds(mine, q2), :] = total * root
    extra[0:1, :] = etotal[0:1, :] * root
    extra[1:8, :] = jnp.broadcast_to(etotal[1:2, :] / live, (7, f))
    scale = 8.0 * (n * n_region * n_dom) / live

    block = sums.at[pl.ds(mine, q2)]
    g2 = [remote(block, block, gsend2.at[k - 1], grecv2.at[k - 1], doms[k - 1]) for k in range(1, n_dom)]
    for copy in g2:
        copy.start()

    for i in range(HALF):
        for j in range(per):
            if i or j:
                halo_copy(i, j).wait()
    tile = 512

    def final_step(t, _):
        part = rows_at(t, tile)
        total = acc[part, :]
        for field in range(HALF):
            ids = jnp.concatenate([hs[p:p + 1, :] for p in range(field * per, (field + 1) * per)], 1)
            got = ret[field * per:(field + 1) * per].reshape(per * halo, f)
            total = total + dot(row_hot(t * tile, tile, ids), got)
        out[part, :] = (total * scale).astype(bf16)
        return 0

    half_tiles = n // tile // 2
    lax.fori_loop(0, half_tiles, final_step, 0)
    for copy in g2:
        copy.wait()
    block = sums.at[pl.ds(core * q0 + chip * q1, q1)]
    g1 = [remote(block, block, gsend1.at[k - 1], grecv1.at[k - 1], chips[k - 1]) for k in range(1, n_chip)]
    for copy in g1:
        copy.start()
    lax.fori_loop(half_tiles, n // tile, final_step, 0)
    for copy in g1:
        copy.wait()
    block = sums.at[pl.ds(core * q0, q0)]
    g0 = remote(block, block, gsend0, grecv0, twin)
    g0.start()
    g0.wait()


def tail(n_region, n_dom, words, agg_grad, base, halo_send, load):
    n, f = agg_grad.shape
    peers, halo = halo_send.shape
    rows = load.shape[0] - 8
    n_chip = n_region // 2
    q0 = rows // 2
    q1 = q0 // n_chip
    q2 = q1 // n_dom
    sem = pltpu.SemaphoreType.DMA
    vm = lambda *dims: pltpu.VMEM(dims, f32)
    blocks = pltpu.VMEM((peers, halo, f), bf16)
    shape = jax.ShapeDtypeStruct
    pairs = [sem, sem, sem((n_chip - 1,)), sem((n_chip - 1,)), sem((n_dom - 1,)), sem((n_dom - 1,))]
    return kernel_call(
        functools.partial(tail_body, n_region, n_dom),
        (shape((n, f), bf16), shape((rows, f), f32), shape((8, f), f32)),
        [vmem()] * 5,
        [
            blocks, blocks, vm(n, f), vm(q0, f), vm(q0, f), vm(n_chip - 1, q1, f), vm(q1, f),
            vm(n_dom - 1, q2, f), vm(8, f), vm(8, f), vm(n_chip - 1, 8, f), vm(8, f), vm(n_dom - 1, 8, f),
            sem((n_dom,)), sem((n_dom,)),
        ] + pairs * 3,
        3, "tail",
    )(words, agg_grad, base, halo_send, load)


def local(
    embeds, neighbours, halo_send, gnn_weight, pair_local, pair_remote, pair_count, targets, pair_w1, pair_w2
):
    f = embeds.shape[1]
    sizes = lax.axis_size("region"), lax.axis_size("dom")
    words, pre, aggregate, nets, asked = head(*sizes, embeds, neighbours, halo_send, pair_remote, gnn_weight)
    sv, sp, small = pair(*sizes, nets, asked, pair_local, targets, pair_count, pair_w1, pair_w2)
    base, agg_grad, load = middle(sv, sp, nets, pre, embeds, aggregate, pair_w1, gnn_weight, small)
    embeds_grad, sums, extra = tail(*sizes, words, agg_grad, base, halo_send, load)
    return embeds_grad, sums[: 2 * f], sums[2 * f :], extra[0], extra[1, 0]


def solution(mesh):
    both = P(("region", "dom"), None)
    in_specs = (both, both, both, P(), both, both, both, both, P(), P())
    out_specs = (both, P(), P(), P(), P())
    return jax.shard_map(local, mesh=mesh, in_specs=in_specs, out_specs=out_specs, check_vma=False)
```

```python
import functools
import jax
import jax.numpy as jnp
from jax import lax
from jax.experimental import pallas as pl
from jax.experimental.pallas import tpu as pltpu
from jax.sharding import PartitionSpec as P

f32 = jnp.float32
bf16 = jnp.bfloat16
gelu_coef = 0.7978845608
contract_rows = (((0,), (0,)), ((), ()))
contract_cols = (((1,), (1,)), ((), ()))
VMEM_LIMIT = 62 * 1024 * 1024
MESH = pl.DeviceIdType.MESH
FIELDS = 8
HALF = FIELDS // 2
HEAD_TILE = 512


def gelu_both(value):
    inner = jnp.tanh(gelu_coef * (value + 0.044715 * value * value * value))
    half = 0.5 * (1.0 + inner)
    slope = half + 0.5 * value * (1.0 - inner * inner) * gelu_coef * (
        1.0 + 3.0 * 0.044715 * value * value
    )
    return value * half, slope


def dot(a, b):
    return jnp.dot(a, b, preferred_element_type=f32)


def dot_rows(a, b):
    return lax.dot_general(a, b, contract_rows, preferred_element_type=f32)


def dot_cols(a, b):
    return lax.dot_general(a, b, contract_cols, preferred_element_type=f32)


def split(value):
    high = value.astype(bf16)
    return high, (value - high.astype(f32)).astype(bf16)


def rows_at(i, tile):
    return pl.ds(pl.multiple_of(i * tile, tile), tile)


def lane_hot(ids, n):
    return (ids == lax.broadcasted_iota(jnp.int32, (ids.shape[0], n), 1)).astype(f32).astype(bf16)


def row_hot(base, tile, ids):
    row = lax.broadcasted_iota(jnp.int32, (tile, ids.shape[1]), 0)
    return (row == ids - base).astype(f32).astype(bf16)


def counts_of(words, field):
    return ((words >> (4 * field)) & 15).astype(f32).astype(bf16)


class Place:
    def __init__(self, n_region, n_dom):
        self.n_region, self.n_dom = n_region, n_dom
        self.n_chip = n_region // 2
        self.per = n_dom // HALF
        self.region = lax.axis_index("region")
        self.dom = lax.axis_index("dom")
        self.chip = self.region // 2
        self.core = lax.rem(self.region, 2)

    def region_to(self, m):
        chip = lax.rem(self.chip + lax.rem(m, self.n_chip), self.n_chip)
        return chip * 2 + lax.rem(self.core + m // self.n_chip, 2)

    def region_from(self, m):
        chip = lax.rem(self.chip + self.n_chip - lax.rem(m, self.n_chip), self.n_chip)
        return chip * 2 + lax.rem(self.core + m // self.n_chip, 2)

    def field_to(self, i):
        return lax.rem(self.dom // self.per + i, HALF)

    def sub_to(self, j):
        return lax.rem(lax.rem(self.dom, self.per) + j, self.per)

    def dom_to(self, k):
        return lax.rem(self.dom + k, self.n_dom)

    def at_region(self, r):
        return (r, self.dom)

    def at_dom(self, d):
        return (self.region, d)


def remote(src, dst, ssem, rsem, device):
    return pltpu.make_async_remote_copy(
        src_ref=src, dst_ref=dst, send_sem=ssem, recv_sem=rsem, device_id=device, device_id_type=MESH
    )


def vmem():
    return pl.BlockSpec(memory_space=pltpu.VMEM)


def smem():
    return pl.BlockSpec(memory_space=pltpu.SMEM)


def kernel_call(body, outs, in_specs, scratch, collective, name, out_specs=None):
    single = not isinstance(outs, tuple)
    specs = vmem() if single else tuple(vmem() for _ in outs)
    params = dict(vmem_limit_bytes=VMEM_LIMIT)
    if collective is not None:
        params.update(collective_id=collective, has_side_effects=True)
    return pl.pallas_call(
        body, out_shape=outs, in_specs=in_specs, out_specs=specs, scratch_shapes=scratch, name=name,
        compiler_params=pltpu.CompilerParams(**params),
    )


def gather_chunk(ids, table, n):
    return dot(lane_hot(ids.T, n), table[...]).astype(bf16)


def step_body(n_region, n_dom, emb, nb, hs, pr, gw, loc, tgt, cnt, w1, w2, out, sums, extra,
              words, wordst, pre, agg, nets, asked, own, hout, recv,
              outgoing, partner, grad, back, va, sv, sp, load, ag, hback, ret,
              r0, s0, r1, s1, r2, e0, ea, e1, eb, e2,
              hsend, hrecv, asend, arecv, fsend, frecv, bsend, brecv, tsend, trecv,
              send0, recv0, send1, recv1, send2, recv2,
              gsend0, grecv0, gsend1, grecv1, gsend2, grecv2, es0, er0, es1, er1, es2, er2):
    place = Place(n_region, n_dom)
    per, n_chip = place.per, place.n_chip
    me, dom, chip, core = place.region, place.dom, place.chip, place.core
    n, f = emb.shape
    h = w1.shape[1]
    halo = hs.shape[1]
    count = loc.shape[1]
    width = words.shape[1]
    wbits = width.bit_length() - 1
    others = ([place.at_dom(place.dom_to(k)) for k in range(1, n_dom)]
              + [place.at_region(place.region_to(m)) for m in range(1, n_region)])
    barrier = pltpu.get_barrier_semaphore()
    for device in others:
        pl.semaphore_signal(barrier, inc=1, device_id=device, device_id_type=MESH)

    def ask(m):
        r = place.region_to(m)
        return remote(pr.at[pl.ds(r, 1)], asked.at[pl.ds(me, 1)], asend.at[m], arecv.at[m], place.at_region(r))

    def halo_copy(i, j):
        p = place.field_to(i) * per + place.sub_to(j)
        return remote(hout.at[p], recv.at[dom], hsend.at[i * per + j], hrecv.at[i * per + j], place.at_dom(p))

    def back_halo(i, j):
        p = place.field_to(i) * per + place.sub_to(j)
        return remote(hback.at[p], ret.at[dom], tsend.at[i * per + j], trecv.at[i * per + j], place.at_dom(p))

    far = [(i, j) for i in range(HALF) for j in range(per) if i or j]

    for i in range(HALF):
        field = place.field_to(i)
        ids = jnp.concatenate([hs[pl.ds(field * per + s, 1), :] for s in range(per)], 1)
        rows = gather_chunk(ids, emb, n)
        for s in range(per):
            hout[field * per + s] = rows[s * halo:(s + 1) * halo]
        if i == 0:
            pl.semaphore_wait(barrier, len(others))
            for m in range(1, n_region):
                ask(m).start()
        for a, b in far:
            if a == i:
                halo_copy(a, b).start()
    recv[dom] = hout[dom]
    asked[pl.ds(me, 1), :] = pr[pl.ds(me, 1), :]

    tile = HEAD_TILE

    def own_step(t, _):
        rows = rows_at(t, tile)
        ids = nb[:, rows].T
        low = ids & (width - 1)
        weight = jnp.left_shift(1, 4 * (ids >> wbits))
        lane = lax.broadcasted_iota(jnp.int32, (tile, width), 1)
        word = jnp.zeros((tile, width), jnp.int32)
        for d in range(ids.shape[1]):
            word = word + jnp.where(lane == low[:, d:d + 1], weight[:, d:d + 1], 0)
        words[rows, :] = word
        acc = jnp.zeros((tile, f), f32)
        for field in range(HALF):
            acc = acc + dot(counts_of(word, field), emb[field * width:(field + 1) * width, :])
        own[rows, :] = acc
        return 0

    lax.fori_loop(0, n // tile, own_step, 0)
    for a, b in far:
        halo_copy(a, b).wait()

    def halo_step(t, _):
        rows = rows_at(t, tile)
        word = words[rows, :]
        acc = own[rows, :]
        for field in range(HALF):
            table = recv[field * per:(field + 1) * per].reshape(width, f)
            acc = acc + dot(counts_of(word, field + HALF), table)
        mean = (acc * 0.125).astype(bf16)
        mine = emb[rows, :]
        lin = dot(mine, gw[:f, :]) + dot(mean, gw[f:, :])
        pre[rows, :] = lin
        agg[rows, :] = mean
        nets[rows, :] = (mine.astype(f32) + gelu_both(lin)[0]).astype(bf16)
        return 0

    lax.fori_loop(0, n // tile, halo_step, 0)
    for m in range(1, n_region):
        ask(m).wait()

    def out_copy(m):
        r = place.region_to(m)
        return remote(outgoing.at[r], partner.at[me], fsend.at[m], frecv.at[m], place.at_region(r))

    def back_copy(m):
        r = place.region_from(m)
        return remote(grad.at[r], back.at[me], bsend.at[m], brecv.at[m], place.at_region(r))

    def gather_step(m, _):
        r = place.region_to(m)
        outgoing[r] = gather_chunk(asked[pl.ds(r, 1), :], nets, n)
        out_copy(m).start()
        return 0

    lax.fori_loop(1, n_region, gather_step, 0)
    partner[me] = gather_chunk(asked[pl.ds(me, 1), :], nets, n)

    def victim_step(q, _):
        va[q] = dot(gather_chunk(loc[pl.ds(q, 1), :], nets, n), w1[:f, :])
        return 0

    lax.fori_loop(0, n_region, victim_step, 0)
    w2f = w2[...].astype(f32).reshape(1, h)
    w2mat = jnp.broadcast_to(w2f, (h, h)).T.astype(bf16)

    rows4 = 4 * f
    load[rows4:, :] = jnp.zeros((8, h), f32)
    live_count = cnt[0, 0]
    for q in range(1, n_region):
        live_count = live_count + cnt[0, q]
    load[rows4 + 2:rows4 + 3, :] = jnp.zeros((1, h), f32) + live_count.astype(f32)

    def pair_step(m):
        q = place.region_from(m)
        linear = va[q] + dot(partner[q], w1[f:, :])
        act, slope = gelu_both(linear)
        act = act.astype(bf16)
        scores = dot(act, w2mat)
        target = tgt[pl.ds(q, 1), :].T
        live = lax.broadcasted_iota(jnp.int32, (count, 1), 0) < cnt[0, q]
        errors = jnp.where(live, scores - target, 0.0)
        residual = 2.0 * errors
        grad[q] = (residual * w2f * slope).astype(bf16)
        load[rows4:rows4 + 1, :] += jnp.sum(residual * act.astype(f32), axis=0, keepdims=True)
        load[rows4 + 1:rows4 + 2, :] += jnp.sum(errors * errors, axis=0, keepdims=True)

    pair_step(0)

    def away_step(m, _):
        out_copy(m).wait_recv()
        pair_step(m)
        back_copy(m).start()
        return 0

    lax.fori_loop(1, n_region, away_step, 0)
    big = 512

    def victim_scatter(t, _):
        total = jnp.zeros((big, h), f32)
        for q in range(n_region):
            total = total + dot(row_hot(t * big, big, loc[q:q + 1, :]), grad[q])
        sv[rows_at(t, big), :] = total
        sp[rows_at(t, big), :] = dot(row_hot(t * big, big, asked[pl.ds(me, 1), :]), grad[me])
        return 0

    lax.fori_loop(0, n // big, victim_scatter, 0)

    def turn(t, _):
        rows = rows_at(t, 256)
        wordst[:, rows] = words[rows, :].T
        return 0

    lax.fori_loop(0, n // 256, turn, 0)

    def partner_scatter(m, _):
        r = place.region_to(m)
        back_copy(m).wait_recv()
        ids = asked[pl.ds(r, 1), :]
        rows_back = back[r]
        for t in range(n // big):
            sp[t * big:(t + 1) * big, :] += dot(row_hot(t * big, big, ids), rows_back)
        return 0

    lax.fori_loop(1, n_region, partner_scatter, 0)

    load[:rows4, :] = jnp.zeros((rows4, f), f32)

    def middle_step(t, _):
        rows = rows_at(t, tile)
        vh, vl = split(sv[rows, :])
        ph, plo = split(sp[rows, :])
        ng = dot_cols(vh, w1[:f, :]) + dot_cols(vl, w1[:f, :]) + dot_cols(ph, w1[f:, :]) + dot_cols(plo, w1[f:, :])
        pg = (ng * gelu_both(pre[rows, :])[1]).astype(bf16)
        own[rows, :] = ng + dot_cols(pg, gw[:f, :])
        ag[rows, :] = (dot_cols(pg, gw[f:, :]) * 0.125).astype(bf16)
        mine = nets[rows, :]
        load[:f, :] += dot_rows(emb[rows, :], pg)
        load[f:2 * f, :] += dot_rows(agg[rows, :], pg)
        load[2 * f:3 * f, :] += dot_rows(mine, vh) + dot_rows(mine, vl)
        load[3 * f:4 * f, :] += dot_rows(mine, ph) + dot_rows(mine, plo)
        return 0

    lax.fori_loop(0, n // tile, middle_step, 0)

    q0 = rows4 // 2
    q1 = q0 // n_chip
    q2 = q1 // n_dom
    twin = place.at_region(chip * 2 + 1 - core)
    chips = [place.at_region(lax.rem(chip + k, n_chip) * 2 + core) for k in range(1, n_chip)]
    doms = [place.at_dom(place.dom_to(k)) for k in range(1, n_dom)]
    c0 = [
        remote(load.at[pl.ds((1 - core) * q0, q0)], r0, send0, recv0, twin),
        remote(load.at[pl.ds(rows4, 8)], e0, es0, er0, twin),
    ]
    for copy in c0:
        copy.start()

    for i in range(HALF):
        field = place.field_to(i)
        part = dot(counts_of(wordst[...], field + HALF), ag[...]).astype(bf16)
        for s in range(per):
            hback[field * per + s] = part[s * halo:(s + 1) * halo]
        for a, b in far:
            if a == i:
                back_halo(a, b).start()
    ret[dom] = hback[dom]

    def own_field(field):
        part = slice(field * width, (field + 1) * width)
        own[part, :] = own[part, :] + dot(counts_of(wordst[...], field), ag[...])

    for copy in c0:
        copy.wait()
    s0[...] = load[pl.ds(core * q0, q0), :] + r0[...]
    ea[...] = load[pl.ds(rows4, 8), :] + e0[...]
    c1 = []
    for k in range(1, n_chip):
        peer = lax.rem(chip + k, n_chip)
        c1.append(remote(s0.at[pl.ds(peer * q1, q1)], r1.at[k - 1], send1.at[k - 1], recv1.at[k - 1], chips[k - 1]))
        c1.append(remote(ea, e1.at[k - 1], es1.at[k - 1], er1.at[k - 1], chips[k - 1]))
    for copy in c1:
        copy.start()
    own_field(0)
    own_field(1)
    for copy in c1:
        copy.wait()
    total = s0[pl.ds(chip * q1, q1), :]
    etotal = ea[...]
    for k in range(1, n_chip):
        total = total + r1[k - 1]
        etotal = etotal + e1[k - 1]
    s1[...] = total
    eb[...] = etotal
    c2 = []
    for k in range(1, n_dom):
        peer = place.dom_to(k)
        c2.append(remote(s1.at[pl.ds(peer * q2, q2)], r2.at[k - 1], send2.at[k - 1], recv2.at[k - 1], doms[k - 1]))
        c2.append(remote(eb, e2.at[k - 1], es2.at[k - 1], er2.at[k - 1], doms[k - 1]))
    for copy in c2:
        copy.start()
    own_field(2)
    own_field(3)
    for copy in c2:
        copy.wait()
    total = s1[pl.ds(dom * q2, q2), :]
    etotal = eb[...]
    for k in range(1, n_dom):
        total = total + r2[k - 1]
        etotal = etotal + e2[k - 1]
    live = etotal[2:3, :]
    root = 8.0 / jnp.sqrt(live)
    mine = core * q0 + chip * q1 + dom * q2
    sums[pl.ds(mine, q2), :] = total * root
    extra[0:1, :] = etotal[0:1, :] * root
    extra[1:8, :] = jnp.broadcast_to(etotal[1:2, :] / live, (7, f))
    scale = 8.0 * (n * n_region * n_dom) / live

    block = sums.at[pl.ds(mine, q2)]
    g2 = [remote(block, block, gsend2.at[k - 1], grecv2.at[k - 1], doms[k - 1]) for k in range(1, n_dom)]
    for copy in g2:
        copy.start()
    for copy in g2:
        copy.wait()
    block1 = sums.at[pl.ds(core * q0 + chip * q1, q1)]
    g1 = [remote(block1, block1, gsend1.at[k - 1], grecv1.at[k - 1], chips[k - 1]) for k in range(1, n_chip)]
    for copy in g1:
        copy.start()
    for a, b in far:
        back_halo(a, b).wait()

    def final_step(t, _):
        part = rows_at(t, big)
        total = own[part, :]
        for field in range(HALF):
            ids = jnp.concatenate([hs[p:p + 1, :] for p in range(field * per, (field + 1) * per)], 1)
            got = ret[field * per:(field + 1) * per].reshape(per * halo, f)
            total = total + dot(row_hot(t * big, big, ids), got)
        out[part, :] = (total * scale).astype(bf16)
        return 0

    lax.fori_loop(0, n // big, final_step, 0)
    for copy in g1:
        copy.wait()
    block0 = sums.at[pl.ds(core * q0, q0)]
    g0 = remote(block0, block0, gsend0, grecv0, twin)
    g0.start()

    def drain(m, _):
        out_copy(m).wait_send()
        back_copy(m).wait_send()
        return 0

    lax.fori_loop(1, n_region, drain, 0)
    g0.wait()


def train_step(n_region, n_dom, emb, nb, hs, pr, gw, loc, tgt, cnt, w1, w2):
    n, f = emb.shape
    h = w1.shape[1]
    peers, halo = hs.shape
    regions, slots = loc.shape
    width = 2 * n // FIELDS
    rows = 4 * f
    n_chip = n_region // 2
    q0 = rows // 2
    q1 = q0 // n_chip
    q2 = q1 // n_dom
    sem = pltpu.SemaphoreType.DMA
    vm = lambda *dims: pltpu.VMEM(dims, f32)
    vb = lambda *dims: pltpu.VMEM(dims, bf16)
    vi = lambda *dims: pltpu.VMEM(dims, jnp.int32)
    shape = jax.ShapeDtypeStruct
    sums_sems = [sem, sem, sem((n_chip - 1,)), sem((n_chip - 1,)), sem((n_dom - 1,)), sem((n_dom - 1,))]
    return kernel_call(
        functools.partial(step_body, n_region, n_dom),
        (shape((n, f), bf16), shape((rows, f), f32), shape((8, f), f32)),
        [vmem()] * 7 + [smem()] + [vmem()] * 2,
        [
            vi(n, width), vi(width, n), vm(n, f), vb(n, f), vb(n, f), vi(regions, slots), vm(n, f),
            vb(peers, halo, f), vb(peers, halo, f),
            vb(regions, slots, f), vb(regions, slots, f), vb(regions, slots, h), vb(regions, slots, h),
            vm(regions, slots, h), vm(n, h), vm(n, h), vm(rows + 8, f), vb(n, f),
            vb(peers, halo, f), vb(peers, halo, f),
            vm(q0, f), vm(q0, f), vm(n_chip - 1, q1, f), vm(q1, f), vm(n_dom - 1, q2, f),
            vm(8, f), vm(8, f), vm(n_chip - 1, 8, f), vm(8, f), vm(n_dom - 1, 8, f),
            sem((n_dom,)), sem((n_dom,)), sem((n_region,)), sem((n_region,)),
            sem((n_region,)), sem((n_region,)), sem((n_region,)), sem((n_region,)), sem((n_dom,)), sem((n_dom,)),
        ] + sums_sems * 3,
        1, "train_step",
    )(emb, nb.T, hs, pr, gw, loc, tgt, cnt, w1, w2)


def finish_body(grad, sums, extra, out, gnn, w1, w2, loss):
    half = gnn.shape[0]
    out[...] = grad[...]
    gnn[...] = sums[:half, :]
    w1[...] = sums[half:, :]
    w2[...] = extra[0:1, :].reshape(w2.shape)
    loss[...] = extra[1:2, 0:1]


def finish(grad, sums, extra):
    rows, f = sums.shape
    shape = jax.ShapeDtypeStruct
    return kernel_call(
        finish_body,
        (shape(grad.shape, bf16), shape((rows // 2, f), f32), shape((rows // 2, f), f32), shape((f,), f32),
         shape((1, 1), f32)),
        [vmem()] * 3, [], None, "finish",
    )(grad, sums, extra)


def local(
    embeds, neighbours, halo_send, gnn_weight, pair_local, pair_remote, pair_count, targets, pair_w1, pair_w2
):
    sizes = lax.axis_size("region"), lax.axis_size("dom")
    outs = train_step(
        *sizes, embeds, neighbours, halo_send, pair_remote, gnn_weight, pair_local, targets, pair_count,
        pair_w1, pair_w2
    )
    *grads, loss = finish(*outs)
    return *grads, loss.reshape(())


def solution(mesh):
    both = P(("region", "dom"), None)
    in_specs = (both, both, both, P(), both, both, both, both, P(), P())
    out_specs = (both, P(), P(), P(), P())
    return jax.shard_map(local, mesh=mesh, in_specs=in_specs, out_specs=out_specs, check_vma=False)
```

```python
import functools
import jax
import jax.numpy as jnp
from jax import lax
from jax.experimental import pallas as pl
from jax.experimental.pallas import tpu as pltpu
from jax.sharding import PartitionSpec as P

f32 = jnp.float32
bf16 = jnp.bfloat16
gelu_coef = 0.7978845608
contract_rows = (((0,), (0,)), ((), ()))
contract_cols = (((1,), (1,)), ((), ()))
VMEM_LIMIT = 62 * 1024 * 1024
MESH = pl.DeviceIdType.MESH
FIELDS = 8
HALF = FIELDS // 2
HEAD_TILE = 512


def gelu_both(value):
    inner = jnp.tanh(gelu_coef * (value + 0.044715 * value * value * value))
    half = 0.5 * (1.0 + inner)
    slope = half + 0.5 * value * (1.0 - inner * inner) * gelu_coef * (
        1.0 + 3.0 * 0.044715 * value * value
    )
    return value * half, slope


def dot(a, b):
    return jnp.dot(a, b, preferred_element_type=f32)


def dot_rows(a, b):
    return lax.dot_general(a, b, contract_rows, preferred_element_type=f32)


def dot_cols(a, b):
    return lax.dot_general(a, b, contract_cols, preferred_element_type=f32)


def split(value):
    high = value.astype(bf16)
    return high, (value - high.astype(f32)).astype(bf16)


def rows_at(i, tile):
    return pl.ds(pl.multiple_of(i * tile, tile), tile)


def lane_hot(ids, n):
    return (ids == lax.broadcasted_iota(jnp.int32, (ids.shape[0], n), 1)).astype(f32).astype(bf16)


def row_hot(base, tile, ids):
    row = lax.broadcasted_iota(jnp.int32, (tile, ids.shape[1]), 0)
    return (row == ids - base).astype(f32).astype(bf16)


def counts_of(words, field):
    return ((words >> (4 * field)) & 15).astype(f32).astype(bf16)


class Place:
    def __init__(self, n_region, n_dom):
        self.n_region, self.n_dom = n_region, n_dom
        self.n_chip = n_region // 2
        self.per = n_dom // HALF
        self.region = lax.axis_index("region")
        self.dom = lax.axis_index("dom")
        self.chip = self.region // 2
        self.core = lax.rem(self.region, 2)

    def region_to(self, m):
        chip = lax.rem(self.chip + lax.rem(m, self.n_chip), self.n_chip)
        return chip * 2 + lax.rem(self.core + m // self.n_chip, 2)

    def region_from(self, m):
        chip = lax.rem(self.chip + self.n_chip - lax.rem(m, self.n_chip), self.n_chip)
        return chip * 2 + lax.rem(self.core + m // self.n_chip, 2)

    def field_to(self, i):
        return lax.rem(self.dom // self.per + i, HALF)

    def sub_to(self, j):
        return lax.rem(lax.rem(self.dom, self.per) + j, self.per)

    def field_from(self, i):
        return lax.rem(self.dom // self.per + HALF - i, HALF)

    def dom_to(self, k):
        return lax.rem(self.dom + k, self.n_dom)

    def at_region(self, r):
        return (r, self.dom)

    def at_dom(self, d):
        return (self.region, d)


def remote(src, dst, ssem, rsem, device):
    return pltpu.make_async_remote_copy(
        src_ref=src, dst_ref=dst, send_sem=ssem, recv_sem=rsem, device_id=device, device_id_type=MESH
    )


def vmem():
    return pl.BlockSpec(memory_space=pltpu.VMEM)


def smem():
    return pl.BlockSpec(memory_space=pltpu.SMEM)


def kernel_call(body, outs, in_specs, scratch, collective, name, out_specs=None):
    single = not isinstance(outs, tuple)
    specs = vmem() if single else tuple(vmem() for _ in outs)
    params = dict(vmem_limit_bytes=VMEM_LIMIT)
    if collective is not None:
        params.update(collective_id=collective, has_side_effects=True)
    return pl.pallas_call(
        body, out_shape=outs, in_specs=in_specs, out_specs=specs, scratch_shapes=scratch, name=name,
        compiler_params=pltpu.CompilerParams(**params),
    )


def gather_chunk(ids, table, n):
    return dot(lane_hot(ids.T, n), table[...]).astype(bf16)


def step_body(n_region, n_dom, emb, nb, hs, pr, gw, loc, tgt, cnt, w1, w2, out, sums, extra,
              words, wordst, pre, agg, nets, asked, own, hout, recv,
              outgoing, partner, grad, back, va, sv, sp, load, ag, hback, ret,
              r0, s0, r1, s1, r2, e0, ea, e1, eb, e2,
              hsend, hrecv, asend, arecv, fsend, frecv, bsend, brecv, tsend, trecv,
              send0, recv0, send1, recv1, send2, recv2,
              gsend0, grecv0, gsend1, grecv1, gsend2, grecv2, es0, er0, es1, er1, es2, er2):
    place = Place(n_region, n_dom)
    per, n_chip = place.per, place.n_chip
    me, dom, chip, core = place.region, place.dom, place.chip, place.core
    n, f = emb.shape
    h = w1.shape[1]
    halo = hs.shape[1]
    count = loc.shape[1]
    width = words.shape[1]
    wbits = width.bit_length() - 1
    others = ([place.at_dom(place.dom_to(k)) for k in range(1, n_dom)]
              + [place.at_region(place.region_to(m)) for m in range(1, n_region)])
    barrier = pltpu.get_barrier_semaphore()
    for device in others:
        pl.semaphore_signal(barrier, inc=1, device_id=device, device_id_type=MESH)

    def ask(m):
        r = place.region_to(m)
        return remote(pr.at[pl.ds(r, 1)], asked.at[pl.ds(me, 1)], asend.at[m], arecv.at[m], place.at_region(r))

    def halo_copy(i, j):
        p = place.field_to(i) * per + place.sub_to(j)
        return remote(hout.at[p], recv.at[dom], hsend.at[i * per + j], hrecv.at[i * per + j], place.at_dom(p))

    def back_halo(i, j):
        p = place.field_to(i) * per + place.sub_to(j)
        return remote(hback.at[p], ret.at[dom], tsend.at[i * per + j], trecv.at[i * per + j], place.at_dom(p))

    far = [(i, j) for i in range(HALF) for j in range(per) if i or j]

    for i in range(HALF):
        field = place.field_to(i)
        ids = jnp.concatenate([hs[pl.ds(field * per + s, 1), :] for s in range(per)], 1)
        rows = gather_chunk(ids, emb, n)
        for s in range(per):
            hout[field * per + s] = rows[s * halo:(s + 1) * halo]
    pl.semaphore_wait(barrier, len(others))
    for m in range(1, n_region):
        ask(m).start()
    for a, b in far:
        halo_copy(a, b).start()
    recv[dom] = hout[dom]
    asked[pl.ds(me, 1), :] = pr[pl.ds(me, 1), :]

    tile = HEAD_TILE

    def own_step(t, _):
        rows = rows_at(t, tile)
        ids = nb[:, rows].T
        low = ids & (width - 1)
        weight = jnp.left_shift(1, 4 * (ids >> wbits))
        lane = lax.broadcasted_iota(jnp.int32, (tile, width), 1)
        word = jnp.zeros((tile, width), jnp.int32)
        for d in range(ids.shape[1]):
            word = word + jnp.where(lane == low[:, d:d + 1], weight[:, d:d + 1], 0)
        words[rows, :] = word
        acc = jnp.zeros((tile, f), f32)
        for field in range(HALF):
            acc = acc + dot(counts_of(word, field), emb[field * width:(field + 1) * width, :])
        own[rows, :] = acc
        return 0

    lax.fori_loop(0, n // tile, own_step, 0)

    def arrived(i):
        for a, b in far:
            if a == i:
                halo_copy(a, b).wait()
        field = place.field_from(i)
        return field + HALF, recv[pl.ds(field * per, per)].reshape(width, f)

    for i in range(HALF - 1):
        field, table = arrived(i)

        def field_step(t, _):
            rows = rows_at(t, tile)
            own[rows, :] += dot(counts_of(words[rows, :], field), table)
            return 0

        lax.fori_loop(0, n // tile, field_step, 0)
    last_field, last_table = arrived(HALF - 1)

    def halo_step(t, _):
        rows = rows_at(t, tile)
        acc = own[rows, :] + dot(counts_of(words[rows, :], last_field), last_table)
        mean = (acc * 0.125).astype(bf16)
        mine = emb[rows, :]
        lin = dot(mine, gw[:f, :]) + dot(mean, gw[f:, :])
        pre[rows, :] = lin
        agg[rows, :] = mean
        nets[rows, :] = (mine.astype(f32) + gelu_both(lin)[0]).astype(bf16)
        return 0

    lax.fori_loop(0, n // tile, halo_step, 0)
    for m in range(1, n_region):
        ask(m).wait()

    def out_copy(m):
        r = place.region_to(m)
        return remote(outgoing.at[r], partner.at[me], fsend.at[m], frecv.at[m], place.at_region(r))

    def back_copy(m):
        r = place.region_from(m)
        return remote(grad.at[r], back.at[me], bsend.at[m], brecv.at[m], place.at_region(r))

    def gather_step(m, _):
        r = place.region_to(m)
        outgoing[r] = gather_chunk(asked[pl.ds(r, 1), :], nets, n)
        out_copy(m).start()
        return 0

    lax.fori_loop(1, n_region, gather_step, 0)
    partner[me] = gather_chunk(asked[pl.ds(me, 1), :], nets, n)

    def victim_step(q, _):
        va[q] = dot(gather_chunk(loc[pl.ds(q, 1), :], nets, n), w1[:f, :])
        return 0

    lax.fori_loop(0, n_region, victim_step, 0)
    w2f = w2[...].astype(f32).reshape(1, h)
    w2mat = jnp.broadcast_to(w2f, (h, h)).T.astype(bf16)

    rows4 = 4 * f
    load[rows4:, :] = jnp.zeros((8, h), f32)
    live_count = cnt[0, 0]
    for q in range(1, n_region):
        live_count = live_count + cnt[0, q]
    load[rows4 + 2:rows4 + 3, :] = jnp.zeros((1, h), f32) + live_count.astype(f32)

    def pair_step(m):
        q = place.region_from(m)
        linear = va[q] + dot(partner[q], w1[f:, :])
        act, slope = gelu_both(linear)
        act = act.astype(bf16)
        scores = dot(act, w2mat)
        target = tgt[pl.ds(q, 1), :].T
        live = lax.broadcasted_iota(jnp.int32, (count, 1), 0) < cnt[0, q]
        errors = jnp.where(live, scores - target, 0.0)
        residual = 2.0 * errors
        grad[q] = (residual * w2f * slope).astype(bf16)
        load[rows4:rows4 + 1, :] += jnp.sum(residual * act.astype(f32), axis=0, keepdims=True)
        load[rows4 + 1:rows4 + 2, :] += jnp.sum(errors * errors, axis=0, keepdims=True)

    pair_step(0)

    def away_step(m, _):
        out_copy(m).wait_recv()
        pair_step(m)
        back_copy(m).start()
        return 0

    lax.fori_loop(1, n_region, away_step, 0)
    big = 512

    def victim_scatter(t, _):
        total = jnp.zeros((big, h), f32)
        for q in range(n_region):
            total = total + dot(row_hot(t * big, big, loc[q:q + 1, :]), grad[q])
        sv[rows_at(t, big), :] = total
        sp[rows_at(t, big), :] = dot(row_hot(t * big, big, asked[pl.ds(me, 1), :]), grad[me])
        return 0

    lax.fori_loop(0, n // big, victim_scatter, 0)

    def turn(t, _):
        rows = rows_at(t, 256)
        wordst[:, rows] = words[rows, :].T
        return 0

    lax.fori_loop(0, n // 256, turn, 0)

    load[:rows4, :] = jnp.zeros((rows4, f), f32)

    def victim_middle(t, _):
        rows = rows_at(t, tile)
        vh, vl = split(sv[rows, :])
        sv[rows, :] = dot_cols(vh, w1[:f, :]) + dot_cols(vl, w1[:f, :])
        load[2 * f:3 * f, :] += dot_rows(nets[rows, :], vh) + dot_rows(nets[rows, :], vl)
        return 0

    lax.fori_loop(0, n // tile, victim_middle, 0)

    def partner_scatter(m, _):
        r = place.region_to(m)
        back_copy(m).wait_recv()
        ids = asked[pl.ds(r, 1), :]
        rows_back = back[r]
        for t in range(n // big):
            sp[t * big:(t + 1) * big, :] += dot(row_hot(t * big, big, ids), rows_back)
        return 0

    lax.fori_loop(1, n_region, partner_scatter, 0)

    def middle_step(t, _):
        rows = rows_at(t, tile)
        ph, plo = split(sp[rows, :])
        ng = sv[rows, :] + dot_cols(ph, w1[f:, :]) + dot_cols(plo, w1[f:, :])
        pg = (ng * gelu_both(pre[rows, :])[1]).astype(bf16)
        own[rows, :] = ng + dot_cols(pg, gw[:f, :])
        ag[rows, :] = (dot_cols(pg, gw[f:, :]) * 0.125).astype(bf16)
        mine = nets[rows, :]
        load[:f, :] += dot_rows(emb[rows, :], pg)
        load[f:2 * f, :] += dot_rows(agg[rows, :], pg)
        load[3 * f:4 * f, :] += dot_rows(mine, ph) + dot_rows(mine, plo)
        return 0

    lax.fori_loop(0, n // tile, middle_step, 0)

    q0 = rows4 // 2
    q1 = q0 // n_chip
    q2 = q1 // n_dom
    twin = place.at_region(chip * 2 + 1 - core)
    chips = [place.at_region(lax.rem(chip + k, n_chip) * 2 + core) for k in range(1, n_chip)]
    doms = [place.at_dom(place.dom_to(k)) for k in range(1, n_dom)]
    chunk0 = [lax.rem(chip + k, n_chip) for k in range(n_chip)]
    c0 = [
        remote(load.at[pl.ds((1 - core) * q0 + chunk0[k] * q1, q1)], r0.at[k], send0.at[k], recv0.at[k], twin)
        for k in range(n_chip)
    ]
    x0 = remote(load.at[pl.ds(rows4, 8)], e0, es0, er0, twin)
    x0.start()
    for k in list(range(1, n_chip)) + [0]:
        c0[k].start()

    for i in range(HALF):
        field = place.field_to(i)
        part = dot(counts_of(wordst[...], field + HALF), ag[...]).astype(bf16)
        for s in range(per):
            hback[field * per + s] = part[s * halo:(s + 1) * halo]
        if i < 2:
            for a, b in far:
                if a == i:
                    back_halo(a, b).start()
    ret[dom] = hback[dom]

    def own_field(field):
        part = slice(field * width, (field + 1) * width)
        own[part, :] = own[part, :] + dot(counts_of(wordst[...], field), ag[...])

    x0.wait()
    ea[...] = load[pl.ds(rows4, 8), :] + e0[...]
    c1 = []
    for k in range(1, n_chip):
        copy = remote(ea, e1.at[k - 1], es1.at[k - 1], er1.at[k - 1], chips[k - 1])
        copy.start()
        c1.append(copy)
    for k in list(range(1, n_chip)) + [0]:
        c0[k].wait()
        s0[k] = load[pl.ds(core * q0 + chunk0[k] * q1, q1), :] + r0[k]
        if k:
            copy = remote(s0.at[k], r1.at[k - 1], send1.at[k - 1], recv1.at[k - 1], chips[k - 1])
            copy.start()
            c1.append(copy)
    for field in range(HALF):
        own_field(field)
    for copy in c1:
        copy.wait()
    total = s0[0]
    etotal = ea[...]
    for k in range(1, n_chip):
        total = total + r1[k - 1]
        etotal = etotal + e1[k - 1]
    s1[...] = total
    eb[...] = etotal
    c2 = []
    for k in range(1, n_dom):
        peer = place.dom_to(k)
        c2.append(remote(s1.at[pl.ds(peer * q2, q2)], r2.at[k - 1], send2.at[k - 1], recv2.at[k - 1], doms[k - 1]))
        c2.append(remote(eb, e2.at[k - 1], es2.at[k - 1], er2.at[k - 1], doms[k - 1]))
    for copy in c2:
        copy.start()
    for a, b in far:
        if a == 2:
            back_halo(a, b).start()
    for copy in c2:
        copy.wait()
    total = s1[pl.ds(dom * q2, q2), :]
    etotal = eb[...]
    for k in range(1, n_dom):
        total = total + r2[k - 1]
        etotal = etotal + e2[k - 1]
    live = etotal[2:3, :]
    root = 8.0 / jnp.sqrt(live)
    base = core * n_chip * n_dom
    mine = base + chip * n_dom + dom
    sums[mine] = (total * root).astype(bf16)
    block = sums.at[pl.ds(mine, 1)]
    g2 = [remote(block, block, gsend2.at[k - 1], grecv2.at[k - 1], doms[k - 1]) for k in range(1, n_dom)]
    for copy in g2:
        copy.start()
    for a, b in far:
        if a == 3:
            back_halo(a, b).start()
    extra[0:1, :] = etotal[0:1, :] * root
    extra[1:8, :] = jnp.broadcast_to(etotal[1:2, :] / live, (7, f))
    scale = 8.0 * (n * n_region * n_dom) / live
    for copy in g2:
        copy.wait()
    block1 = sums.at[pl.ds(base + chip * n_dom, n_dom)]
    g1 = [remote(block1, block1, gsend1.at[k - 1], grecv1.at[k - 1], chips[k - 1]) for k in range(1, n_chip)]
    for copy in g1:
        copy.start()

    def across(k):
        part = sums.at[pl.ds(base + lax.rem(chip + n_chip - k, n_chip) * n_dom, n_dom)]
        return remote(part, part, gsend0.at[k], grecv0.at[k], twin)

    g0 = [across(k) for k in range(n_chip)]
    g0[0].start()
    for a, b in far:
        back_halo(a, b).wait()

    def final_step(t, _):
        part = rows_at(t, big)
        total = own[part, :]
        for field in range(HALF):
            ids = jnp.concatenate([hs[p:p + 1, :] for p in range(field * per, (field + 1) * per)], 1)
            got = ret[field * per:(field + 1) * per].reshape(per * halo, f)
            total = total + dot(row_hot(t * big, big, ids), got)
        out[part, :] = (total * scale).astype(bf16)
        return 0

    lax.fori_loop(0, n // big, final_step, 0)
    for k in range(1, n_chip):
        g1[k - 1].wait()
        g0[k].start()

    def drain(m, _):
        out_copy(m).wait_send()
        back_copy(m).wait_send()
        return 0

    lax.fori_loop(1, n_region, drain, 0)
    for copy in g0:
        copy.wait()


def train_step(n_region, n_dom, emb, nb, hs, pr, gw, loc, tgt, cnt, w1, w2):
    n, f = emb.shape
    h = w1.shape[1]
    peers, halo = hs.shape
    regions, slots = loc.shape
    width = 2 * n // FIELDS
    rows = 4 * f
    n_chip = n_region // 2
    q0 = rows // 2
    q1 = q0 // n_chip
    q2 = q1 // n_dom
    sem = pltpu.SemaphoreType.DMA
    vm = lambda *dims: pltpu.VMEM(dims, f32)
    vb = lambda *dims: pltpu.VMEM(dims, bf16)
    vi = lambda *dims: pltpu.VMEM(dims, jnp.int32)
    shape = jax.ShapeDtypeStruct
    sums_sems = [sem((n_chip,)), sem((n_chip,)), sem((n_chip - 1,)), sem((n_chip - 1,)), sem((n_dom - 1,)), sem((n_dom - 1,))]
    return kernel_call(
        functools.partial(step_body, n_region, n_dom),
        (shape((n, f), bf16), shape((rows // q2, q2, f), bf16), shape((8, f), f32)),
        [vmem()] * 7 + [smem()] + [vmem()] * 2,
        [
            vi(n, width), vi(width, n), vm(n, f), vb(n, f), vb(n, f), vi(regions, slots), vm(n, f),
            vb(peers, halo, f), vb(peers, halo, f),
            vb(regions, slots, f), vb(regions, slots, f), vb(regions, slots, h), vb(regions, slots, h),
            vm(regions, slots, h), vm(n, h), vm(n, h), vm(rows + 8, f), vb(n, f),
            vb(peers, halo, f), vb(peers, halo, f),
            vm(n_chip, q1, f), vm(n_chip, q1, f), vm(n_chip - 1, q1, f), vm(q1, f), vm(n_dom - 1, q2, f),
            vm(8, f), vm(8, f), vm(n_chip - 1, 8, f), vm(8, f), vm(n_dom - 1, 8, f),
            sem((n_dom,)), sem((n_dom,)), sem((n_region,)), sem((n_region,)),
            sem((n_region,)), sem((n_region,)), sem((n_region,)), sem((n_region,)), sem((n_dom,)), sem((n_dom,)),
        ] + sums_sems * 2 + [sem, sem] + sums_sems[2:],
        1, "train_step",
    )(emb, nb.T, hs, pr, gw, loc, tgt, cnt, w1, w2)


def finish_body(grad, sums, extra, out, gnn, w1, w2, loss):
    half = sums.shape[0] // 2
    out[...] = grad[...]
    gnn[...] = sums[:half].reshape(gnn.shape).astype(f32)
    w1[...] = sums[half:].reshape(w1.shape).astype(f32)
    w2[...] = extra[0:1, :].reshape(w2.shape)
    loss[...] = extra[1:2, 0:1]


def finish(grad, sums, extra):
    f = sums.shape[2]
    rows = sums.shape[0] * sums.shape[1]
    shape = jax.ShapeDtypeStruct
    return kernel_call(
        finish_body,
        (shape(grad.shape, bf16), shape((rows // 2, f), f32), shape((rows // 2, f), f32), shape((f,), f32),
         shape((1, 1), f32)),
        [vmem()] * 3, [], None, "finish",
    )(grad, sums, extra)


def local(
    embeds, neighbours, halo_send, gnn_weight, pair_local, pair_remote, pair_count, targets, pair_w1, pair_w2
):
    sizes = lax.axis_size("region"), lax.axis_size("dom")
    outs = train_step(
        *sizes, embeds, neighbours, halo_send, pair_remote, gnn_weight, pair_local, targets, pair_count,
        pair_w1, pair_w2
    )
    *grads, loss = finish(*outs)
    return *grads, loss.reshape(())


def solution(mesh):
    both = P(("region", "dom"), None)
    in_specs = (both, both, both, P(), both, both, both, both, P(), P())
    out_specs = (both, P(), P(), P(), P())
    return jax.shard_map(local, mesh=mesh, in_specs=in_specs, out_specs=out_specs, check_vma=False)
```
